256 devices in a mesh: seq: 16 (over y_lo, x, core), tp: 16 (over z, y_hi).
Axes of the slice: x: 4, y: 4 (y_hi: 2, y_lo: 2; y = y_hi * 2 + y_lo), z: 8, core: 2. Of those that a mesh axis runs over, the one named last changes fastest.
Arguments:
- tokens: bfloat16 [4096, 5376], P('seq', 'tp'), may hold values from -24 to 24
- w_query: bfloat16 [5376, 4096], P('seq', 'tp'), may hold values from -0.078125 to 0.078125
- w_key: bfloat16 [5376, 2048], P('seq', 'tp'), may hold values from -0.078125 to 0.078125
- w_value: bfloat16 [5376, 2048], P('seq', 'tp'), may hold values from -0.078125 to 0.078125
- w_out: bfloat16 [4096, 5376], P('tp', 'seq'), may hold values from -0.09375 to 0.09375
- cotangent: bfloat16 [4096, 5376], P('seq', 'tp'), may hold values from -6 to 6
- block_lists: int32 [32, 9], P('seq'), may hold values from -1 to 31, as said below
Outputs:
- grad_tokens: bfloat16 [4096, 5376], P('seq', 'tp')
- grad_query: bfloat16 [5376, 4096], P('seq', 'tp')
- grad_key: bfloat16 [5376, 2048], P('seq', 'tp')
- grad_value: bfloat16 [5376, 2048], P('seq', 'tp')
- grad_w_out: bfloat16 [4096, 5376], P('tp', 'seq')
The draws below stay inside these ranges and needn't reach their ends.
Inputs may be any that keep to these rules, and one draw needn't show every extreme that they name: `block_lists`: entry k of query block b is b - 8 + k if that key block lies in the same document as block b, else -1. Documents are runs of whole blocks; the last entry of each row is b, and the valid entries of a row are its last ones.
All inputs are finite; a program needn't handle non-finite values.
Results may differ from the reference program's by a relative error of at most 0.025.
Values may be sent and summed in bfloat16 or wider, within the bound.
No kernel may reach another device: no remote copies, remote signals or barrier semaphores. Data moves between devices by JAX's collectives and lax.ppermute only.
A program may use at most 64 MiB of HBM per device.

```python
import jax
import jax.numpy as jnp
from jax import lax

D = 5376
HEADS = 32
KV_HEADS = 16
HD = 128
WIN = 1024
TOK_DEV = 256
TOKENS = 4096
NQB = 32
LIST = 9
ATTN_SCALAR = 168


def draw_tokens(key, part):
    normal_vals = jnp.clip(jax.random.normal(key, (TOKENS, D), jnp.float32), -6.0, 6.0)
    return normal_vals.astype(jnp.bfloat16)


def draw_block_lists(key, part):
    flags = jax.random.randint(jax.random.fold_in(key, 3), (NQB,), 0, 8)
    block_ids = jnp.arange(NQB, dtype=jnp.int32)
    starts = jnp.where(flags == 0, block_ids, 0).astype(jnp.int32)
    doc_start = lax.cummax(starts, axis=0)
    offsets = jnp.arange(LIST, dtype=jnp.int32) - (LIST - 1)
    wanted = block_ids[:, None] + offsets[None, :]
    valid = wanted >= doc_start[:, None]
    return jnp.where(valid, wanted, -1).astype(jnp.int32)


def shard_levels(rng, shape, shards, smallest, high):
    level, own = 1.0, jax.random.fold_in(rng, 6)
    for axis_at, parts in shards:
        steps = jnp.exp(jax.random.uniform(jax.random.fold_in(own, axis_at), (parts,), jnp.float32, smallest / len(shards), high / len(shards)))
        level = level * jnp.repeat(steps, shape[axis_at] // parts).reshape([-1 if axis == axis_at else 1 for axis in range(len(shape))])
    return level


def centred(rng, extent, spread, limit, shards=(), kind=jnp.bfloat16):
    gain = shard_levels(rng, extent, shards, -0.22, 0.18) if shards else 1.0
    entries = jax.random.normal(rng, extent, jnp.float32) * spread * gain
    return jnp.minimum(jnp.maximum(entries, -limit), limit).astype(kind)


def setup_inputs(seed: int = 0) -> dict:
    key_list = jax.random.split(jax.random.key(seed), 8)
    return {
        "tokens": draw_tokens(jax.random.fold_in(key_list[7], 71), 0),
        "w_query": centred(key_list[1], (D, HEADS * HD), D ** -0.5, 0.078125, ((0, 16), (1, 16))),
        "w_key": centred(key_list[2], (D, KV_HEADS * HD), D ** -0.5, 0.078125, ((0, 16), (1, 16))),
        "w_value": centred(key_list[3], (D, KV_HEADS * HD), D ** -0.5, 0.078125, ((0, 16), (1, 16))),
        "w_out": centred(key_list[4], (HEADS * HD, D), (HEADS * HD) ** -0.5, 0.09375, ((0, 16), (1, 16))),
        "cotangent": centred(key_list[5], (TOKENS, D), 1.0, 6.0, ((0, 16), (1, 16))),
        "block_lists": draw_block_lists(jax.random.fold_in(key_list[7], 71), 0),
    }


def window_view(blocks, n_blocks, span):
    return jnp.concatenate([blocks[offset:offset + n_blocks] for offset in range(span)], axis=1)


def fold_windows(windows, n_blocks, span, block_len):
    shaped = windows.reshape(n_blocks, span, block_len, windows.shape[2], windows.shape[3])
    summed = jnp.zeros((n_blocks + span - 1, block_len, windows.shape[2], windows.shape[3]), jnp.float32)
    for offset in range(span):
        summed = summed.at[offset:offset + n_blocks].add(shaped[:, offset])
    return summed.reshape((n_blocks + span - 1) * block_len, windows.shape[2] * windows.shape[3])


def local_attention(query, keys, values, d_attn, block_lists, softmax_scale):
    tok_rows, kv_local, group_size, head_dim = query.shape
    n_blocks, span = block_lists.shape
    block_len = tok_rows // n_blocks
    width = span * block_len
    key_blocks = keys.reshape(n_blocks + span - 1, block_len, kv_local, head_dim)
    val_blocks = values.reshape(n_blocks + span - 1, block_len, kv_local, head_dim)
    key_win = window_view(key_blocks, n_blocks, span).astype(jnp.float32)
    val_win = window_view(val_blocks, n_blocks, span).astype(jnp.float32)
    q_blocks = query.reshape(n_blocks, block_len, kv_local, group_size, head_dim).astype(jnp.float32)
    grad_blocks = d_attn.reshape(n_blocks, block_len, kv_local, group_size, head_dim).astype(jnp.float32)
    scores = jnp.einsum("btkgd,bwkd->bkgtw", q_blocks, key_win) * softmax_scale
    rows_at = jnp.arange(block_len)[:, None]
    cols_at = jnp.arange(width)[None, :]
    inside = (cols_at > rows_at) & (cols_at <= rows_at + (width - block_len))
    listed = jnp.repeat(block_lists >= 0, block_len, axis=1)
    allowed = inside[None, None, None] & listed[:, None, None, None, :]
    masked = jnp.where(allowed, scores, -1e30)
    highest = jnp.max(masked, axis=-1, keepdims=True)
    weights = jnp.where(allowed, jnp.exp(masked - highest), 0.0)
    probs = weights / jnp.sum(weights, axis=-1, keepdims=True)
    probs_half = probs.astype(jnp.bfloat16).astype(jnp.float32)
    attn = jnp.einsum("bkgtw,bwkd->btkgd", probs_half, val_win).astype(jnp.bfloat16)
    delta = jnp.sum(grad_blocks * attn.astype(jnp.float32), axis=-1)
    delta = jnp.transpose(delta, (0, 2, 3, 1))[..., None]
    grad_probs = jnp.einsum("btkgd,bwkd->bkgtw", grad_blocks, val_win)
    grad_scores = (probs * (grad_probs - delta)).astype(jnp.bfloat16).astype(jnp.float32)
    grad_q = (jnp.einsum("bkgtw,bwkd->btkgd", grad_scores, key_win) * softmax_scale).astype(jnp.bfloat16)
    grad_kwin = jnp.einsum("bkgtw,btkgd->bwkd", grad_scores, q_blocks) * softmax_scale
    grad_vwin = jnp.einsum("bkgtw,btkgd->bwkd", probs_half, grad_blocks)
    grad_keys = fold_windows(grad_kwin, n_blocks, span, block_len)
    grad_values = fold_windows(grad_vwin, n_blocks, span, block_len)
    flat = kv_local * group_size * head_dim
    return attn.reshape(tok_rows, flat), grad_q.reshape(tok_rows, flat), grad_keys, grad_values


def grouped(left, right):
    left_groups = left.reshape(TOKENS // TOK_DEV, TOK_DEV, left.shape[1])
    right_groups = right.reshape(TOKENS // TOK_DEV, TOK_DEV, right.shape[1])

    def add_group(summed, operands):
        term = jnp.dot(operands[0].T, operands[1], preferred_element_type=jnp.float32)
        rounded = lax.optimization_barrier(term.astype(jnp.bfloat16))
        return summed + rounded.astype(jnp.float32), None

    start_sum = jnp.zeros((left.shape[1], right.shape[1]), jnp.float32)
    summed, _ = lax.scan(add_group, start_sum, (left_groups, right_groups))
    return summed.astype(jnp.bfloat16)


def reference(tokens, w_query, w_key, w_value, w_out, cotangent, block_lists):
    softmax_scale = ATTN_SCALAR ** -0.5
    group_size = HEADS // KV_HEADS
    query = jnp.dot(tokens, w_query, preferred_element_type=jnp.float32).astype(jnp.bfloat16)
    keys = jnp.dot(tokens, w_key, preferred_element_type=jnp.float32).astype(jnp.bfloat16)
    values = jnp.dot(tokens, w_value, preferred_element_type=jnp.float32).astype(jnp.bfloat16)
    d_attn = jnp.dot(cotangent, w_out.T, preferred_element_type=jnp.float32).astype(jnp.bfloat16)
    leading = jnp.zeros((WIN, KV_HEADS * HD), jnp.bfloat16)
    key_pad = jnp.concatenate([leading, keys], axis=0)
    val_pad = jnp.concatenate([leading, values], axis=0)
    q_heads = query.reshape(TOKENS, KV_HEADS, 1, group_size, HD).transpose(1, 0, 2, 3, 4)
    d_heads = d_attn.reshape(TOKENS, KV_HEADS, 1, group_size, HD).transpose(1, 0, 2, 3, 4)
    k_heads = key_pad.reshape(WIN + TOKENS, KV_HEADS, 1, HD).transpose(1, 0, 2, 3)
    v_heads = val_pad.reshape(WIN + TOKENS, KV_HEADS, 1, HD).transpose(1, 0, 2, 3)

    def one_head(operands):
        return local_attention(operands[0], operands[1], operands[2], operands[3], block_lists, softmax_scale)

    attn, grad_q, grad_k, grad_v = lax.map(one_head, (q_heads, k_heads, v_heads, d_heads))
    attn = attn.transpose(1, 0, 2).reshape(TOKENS, HEADS * HD)
    grad_q = grad_q.transpose(1, 0, 2).reshape(TOKENS, HEADS * HD)
    grad_k = grad_k[:, WIN:].transpose(1, 0, 2).reshape(TOKENS, KV_HEADS * HD).astype(jnp.bfloat16)
    grad_v = grad_v[:, WIN:].transpose(1, 0, 2).reshape(TOKENS, KV_HEADS * HD).astype(jnp.bfloat16)
    grad_tokens = (jnp.dot(grad_q, w_query.T, preferred_element_type=jnp.float32)
                   + jnp.dot(grad_k, w_key.T, preferred_element_type=jnp.float32)
                   + jnp.dot(grad_v, w_value.T, preferred_element_type=jnp.float32)).astype(jnp.bfloat16)
    grad_query = grouped(tokens, grad_q)
    grad_key = grouped(tokens, grad_k)
    grad_value = grouped(tokens, grad_v)
    grad_w_out = grouped(attn, cotangent)
    return (grad_tokens, grad_query, grad_key, grad_value, grad_w_out)
```

```python
import jax
import jax.numpy as jnp
from jax import lax
from jax.sharding import Mesh
from jax.sharding import PartitionSpec as P

HEADS = 32
KV_HEADS = 16
HD = 128
WIN = 1024
ATTN_SCALAR = 168

SEQ = ("ylo", "x", "core")
TP = ("z", "yhi")
SEQ_SPLIT = (2, 4, 2)
TP_SPLIT = (8, 2)


def from_behind(block, axis, distance):
    devices = range(lax.psum(1, axis))
    route = [(i - distance, i) for i in devices if i - distance in devices]
    return lax.ppermute(block, axis, route)


def window_view(blocks, n_blocks, span):
    return jnp.concatenate([blocks[offset : offset + n_blocks] for offset in range(span)], axis=1)


def fold_windows(windows, n_blocks, span, block_len):
    shaped = windows.reshape(n_blocks, span, block_len, windows.shape[2], windows.shape[3])
    summed = jnp.zeros(
        (n_blocks + span - 1, block_len, windows.shape[2], windows.shape[3]), jnp.float32
    )
    for offset in range(span):
        summed = summed.at[offset : offset + n_blocks].add(shaped[:, offset])
    return summed.reshape((n_blocks + span - 1) * block_len, windows.shape[2] * windows.shape[3])


def local_attention(query, keys, values, d_attn, block_lists, softmax_scale):
    tok_rows, kv_local, group_size, head_dim = query.shape
    n_blocks, span = block_lists.shape
    block_len = tok_rows // n_blocks
    width = span * block_len
    key_blocks = keys.reshape(n_blocks + span - 1, block_len, kv_local, head_dim)
    val_blocks = values.reshape(n_blocks + span - 1, block_len, kv_local, head_dim)
    key_win = window_view(key_blocks, n_blocks, span)
    val_win = window_view(val_blocks, n_blocks, span)
    q_blocks = query.reshape(n_blocks, block_len, kv_local, group_size, head_dim)
    grad_blocks = d_attn.reshape(n_blocks, block_len, kv_local, group_size, head_dim)
    scores = (
        jnp.einsum("btkgd,bwkd->bkgtw", q_blocks, key_win, preferred_element_type=jnp.float32)
        * softmax_scale
    )
    rows_at = jnp.arange(block_len)[:, None]
    cols_at = jnp.arange(width)[None, :]
    inside = (cols_at > rows_at) & (cols_at <= rows_at + (width - block_len))
    listed = jnp.repeat(block_lists >= 0, block_len, axis=1)
    allowed = inside[None, None, None] & listed[:, None, None, None, :]
    masked = jnp.where(allowed, scores, -1e30)
    highest = jnp.max(masked, axis=-1, keepdims=True)
    weights = jnp.where(allowed, jnp.exp(masked - highest), 0.0)
    probs = weights / jnp.sum(weights, axis=-1, keepdims=True)
    probs_half = probs.astype(jnp.bfloat16)
    attn = jnp.einsum(
        "bkgtw,bwkd->btkgd", probs_half, val_win, preferred_element_type=jnp.float32
    ).astype(jnp.bfloat16)
    delta = jnp.sum(grad_blocks.astype(jnp.float32) * attn.astype(jnp.float32), axis=-1)
    delta = jnp.transpose(delta, (0, 2, 3, 1))[..., None]
    grad_probs = jnp.einsum(
        "btkgd,bwkd->bkgtw", grad_blocks, val_win, preferred_element_type=jnp.float32
    )
    grad_scores = (probs * (grad_probs - delta)).astype(jnp.bfloat16)
    grad_q = (
        jnp.einsum("bkgtw,bwkd->btkgd", grad_scores, key_win, preferred_element_type=jnp.float32)
        * softmax_scale
    ).astype(jnp.bfloat16)
    grad_kwin = (
        jnp.einsum("bkgtw,btkgd->bwkd", grad_scores, q_blocks, preferred_element_type=jnp.float32)
        * softmax_scale
    )
    grad_vwin = jnp.einsum(
        "bkgtw,btkgd->bwkd", probs_half, grad_blocks, preferred_element_type=jnp.float32
    )
    grad_keys = fold_windows(grad_kwin, n_blocks, span, block_len)
    grad_values = fold_windows(grad_vwin, n_blocks, span, block_len)
    flat = kv_local * group_size * head_dim
    return (attn.reshape(tok_rows, flat), grad_q.reshape(tok_rows, flat), grad_keys, grad_values)


def contract_cols(left, right):
    return lax.dot_general(
        left, right, (((1,), (1,)), ((), ())), preferred_element_type=jnp.float32
    )


def term_maker(left, right):
    return lax.dot_general(
        left, right, (((0,), (0,)), ((), ())), preferred_element_type=jnp.float32
    )


def shards(tokens, w_query, w_key, w_value, w_out, cotangent, block_lists):
    softmax_scale = ATTN_SCALAR ** (-0.5)
    group_size = HEADS // KV_HEADS
    head_dim = HD
    tok_rows = tokens.shape[0]
    reach = WIN // tok_rows
    n_q = w_query.shape[1]
    n_kv = w_key.shape[1]
    n_proj = n_q + 2 * n_kv
    pair = jnp.stack([tokens, cotangent])
    pair = lax.all_gather(pair, "yhi", axis=2, tiled=True)
    pair = lax.all_gather(pair, "z", axis=2, tiled=True)
    full_tokens, full_cot = pair[0], pair[1]
    w_cat = jnp.concatenate([w_query, w_key, w_value, w_out.T], axis=1)
    w_full = lax.all_gather(w_cat, SEQ, axis=0, tiled=True)
    proj_full = w_full[:, :n_proj]
    d_attn = jnp.dot(full_cot, w_full[:, n_proj:], preferred_element_type=jnp.float32).astype(
        jnp.bfloat16
    )
    qkv = jnp.dot(full_tokens, proj_full, preferred_element_type=jnp.float32).astype(jnp.bfloat16)
    query = qkv[:, :n_q]
    keys = qkv[:, n_q : n_q + n_kv]
    values = qkv[:, n_q + n_kv :]
    earlier = [from_behind((keys, values), SEQ, distance) for distance in range(reach, 0, -1)]
    key_ext = jnp.concatenate([member[0] for member in earlier] + [keys], axis=0)
    value_ext = jnp.concatenate([member[1] for member in earlier] + [values], axis=0)
    kv_local = keys.shape[1] // head_dim
    attn, grad_q, grad_k_ext, grad_v_ext = local_attention(
        query.reshape(tok_rows, kv_local, group_size, head_dim),
        key_ext.reshape(-1, kv_local, head_dim),
        value_ext.reshape(-1, kv_local, head_dim),
        d_attn.reshape(tok_rows, kv_local, group_size, head_dim),
        block_lists,
        softmax_scale,
    )

    def segment(array, index):
        return array[index * tok_rows : (index + 1) * tok_rows]

    summed_k = segment(grad_k_ext, reach)
    summed_v = segment(grad_v_ext, reach)
    for distance in range(1, reach + 1):
        back_k, back_v = from_behind(
            (segment(grad_k_ext, reach - distance), segment(grad_v_ext, reach - distance)),
            SEQ,
            -distance,
        )
        summed_k = summed_k + back_k
        summed_v = summed_v + back_v
    grad_k = summed_k.astype(jnp.bfloat16)
    grad_v = summed_v.astype(jnp.bfloat16)
    grad_act = jnp.concatenate([grad_q, grad_k, grad_v], axis=1)
    token_term = contract_cols(grad_act, proj_full).astype(jnp.bfloat16)
    n_tp = lax.psum(1, TP)
    cols = token_term.shape[1] // n_tp
    parts = lax.all_to_all(token_term.reshape(tok_rows, n_tp, cols), TP, 1, 1, tiled=True)
    grad_tokens = parts.astype(jnp.float32).sum(axis=1).astype(jnp.bfloat16)
    weight_terms = jnp.concatenate(
        [
            term_maker(full_tokens, grad_act).astype(jnp.bfloat16),
            term_maker(full_cot, attn).astype(jnp.bfloat16),
        ],
        axis=1,
    )
    summed = lax.psum_scatter(weight_terms, SEQ, scatter_dimension=0, tiled=True)
    grad_query = summed[:, :n_q]
    grad_key = summed[:, n_q : n_q + n_kv]
    grad_value = summed[:, n_q + n_kv : n_proj]
    grad_w_out = summed[:, n_proj:].T
    return (grad_tokens, grad_query, grad_key, grad_value, grad_w_out)


def solution(mesh):
    fine = Mesh(mesh.devices.reshape(SEQ_SPLIT + TP_SPLIT), SEQ + TP)
    in_specs = (
        P(SEQ, TP),
        P(SEQ, TP),
        P(SEQ, TP),
        P(SEQ, TP),
        P(TP, SEQ),
        P(SEQ, TP),
        P(SEQ, None),
    )
    out_specs = (P(SEQ, TP), P(SEQ, TP), P(SEQ, TP), P(SEQ, TP), P(TP, SEQ))
    return jax.shard_map(shards, mesh=fine, in_specs=in_specs, out_specs=out_specs, check_vma=False)
```

```python
import functools

import jax
import jax.numpy as jnp
from jax import lax
from jax.experimental import pallas as pl
from jax.sharding import Mesh
from jax.sharding import PartitionSpec as P

HEADS = 32
KV_HEADS = 16
HD = 128
WIN = 1024
ATTN_SCALAR = 168

SEQ = ("ylo", "x", "core")
TP = ("z", "yhi")
SEQ_SPLIT = (2, 4, 2)
TP_SPLIT = (8, 2)


def from_behind(block, axis, distance):
    devices = range(lax.psum(1, axis))
    route = [(i - distance, i) for i in devices if i - distance in devices]
    return lax.ppermute(block, axis, route)


def _nt(left, right):
    return lax.dot_general(left, right, (((1,), (1,)), ((), ())), preferred_element_type=jnp.float32)


def _nn(left, right):
    return lax.dot_general(left, right, (((1,), (0,)), ((), ())), preferred_element_type=jnp.float32)


def attention_kernel(q_ref, d_ref, kv_ref, lst_ref, attn_ref, gq_ref, dkv_ref, *, scale, block_len, span, head_dim):
    n_blocks = q_ref.shape[0] // block_len
    groups = q_ref.shape[1] // head_dim
    width = span * block_len
    dkv_ref[...] = jnp.zeros(dkv_ref.shape, jnp.float32)
    rows = lax.broadcasted_iota(jnp.int32, (block_len, width), 0)
    cols = lax.broadcasted_iota(jnp.int32, (block_len, width), 1)
    inside = (cols > rows) & (cols <= rows + (width - block_len))
    for b in range(n_blocks):
        w0 = b * block_len
        kw = kv_ref[w0 : w0 + width, :head_dim]
        vw = kv_ref[w0 : w0 + width, head_dim:]
        allowed = inside & (lst_ref[b : b + 1, :] > 0.0)
        dk_acc = jnp.zeros((width, head_dim), jnp.float32)
        dv_acc = jnp.zeros((width, head_dim), jnp.float32)
        for g in range(groups):
            r0, c0 = b * block_len, g * head_dim
            qb = q_ref[r0 : r0 + block_len, c0 : c0 + head_dim]
            db = d_ref[r0 : r0 + block_len, c0 : c0 + head_dim]
            scores = _nt(qb, kw) * scale
            masked = jnp.where(allowed, scores, -1e30)
            highest = jnp.max(masked, axis=1, keepdims=True)
            weights = jnp.where(allowed, jnp.exp(masked - highest), 0.0)
            probs = weights / jnp.sum(weights, axis=1, keepdims=True)
            probs_half = probs.astype(jnp.bfloat16)
            attn = _nn(probs_half, vw).astype(jnp.bfloat16)
            attn_ref[r0 : r0 + block_len, c0 : c0 + head_dim] = attn
            delta = jnp.sum(db.astype(jnp.float32) * attn.astype(jnp.float32), axis=1, keepdims=True)
            grad_probs = _nt(db, vw)
            grad_scores = (probs * (grad_probs - delta)).astype(jnp.bfloat16)
            grad_q = _nn(grad_scores, kw) * scale
            gq_ref[r0 : r0 + block_len, c0 : c0 + head_dim] = grad_q.astype(jnp.bfloat16)
            dk_acc = dk_acc + _nn(grad_scores.T, qb)
            dv_acc = dv_acc + _nn(probs_half.T, db)
        dkv_ref[w0 : w0 + width, :head_dim] += dk_acc * scale
        dkv_ref[w0 : w0 + width, head_dim:] += dv_acc


def fused_attention(query, kv_ext, d_attn, block_lists, scale, head_dim):
    n_blocks, span = block_lists.shape
    block_len = query.shape[0] // n_blocks
    listed = jnp.repeat((block_lists >= 0).astype(jnp.float32), block_len, axis=1)
    body = functools.partial(
        attention_kernel, scale=scale, block_len=block_len, span=span, head_dim=head_dim
    )
    return pl.pallas_call(
        body,
        out_shape=(
            jax.ShapeDtypeStruct(query.shape, jnp.bfloat16),
            jax.ShapeDtypeStruct(query.shape, jnp.bfloat16),
            jax.ShapeDtypeStruct(kv_ext.shape, jnp.float32),
        ),
    )(query, d_attn, kv_ext, listed)


def contract_cols(left, right):
    return lax.dot_general(
        left, right, (((1,), (1,)), ((), ())), preferred_element_type=jnp.float32
    )


def term_maker(left, right):
    return lax.dot_general(
        left, right, (((0,), (0,)), ((), ())), preferred_element_type=jnp.float32
    )


def shards(tokens, w_query, w_key, w_value, w_out, cotangent, block_lists):
    softmax_scale = ATTN_SCALAR ** (-0.5)
    head_dim = HD
    tok_rows = tokens.shape[0]
    reach = WIN // tok_rows
    n_q = w_query.shape[1]
    n_kv = w_key.shape[1]
    n_proj = n_q + 2 * n_kv
    pair = jnp.stack([tokens, cotangent])
    pair = lax.all_gather(pair, "yhi", axis=2, tiled=True)
    pair = lax.all_gather(pair, "z", axis=2, tiled=True)
    full_tokens, full_cot = pair[0], pair[1]
    w_cat = jnp.concatenate([w_query, w_key, w_value, w_out.T], axis=1)
    w_full = lax.all_gather(w_cat, SEQ, axis=0, tiled=True)
    proj_full = w_full[:, :n_proj]
    d_attn = jnp.dot(full_cot, w_full[:, n_proj:], preferred_element_type=jnp.float32).astype(
        jnp.bfloat16
    )
    qkv = jnp.dot(full_tokens, proj_full, preferred_element_type=jnp.float32).astype(jnp.bfloat16)
    query = qkv[:, :n_q]
    kv = qkv[:, n_q:]
    earlier = [from_behind(kv, SEQ, distance) for distance in range(reach, 0, -1)]
    kv_ext = jnp.concatenate(earlier + [kv], axis=0)
    attn, grad_q, grad_kv_ext = fused_attention(
        query, kv_ext, d_attn, block_lists, softmax_scale, head_dim
    )

    def segment(array, index):
        return array[index * tok_rows : (index + 1) * tok_rows]

    summed_kv = segment(grad_kv_ext, reach)
    for distance in range(1, reach + 1):
        summed_kv = summed_kv + from_behind(segment(grad_kv_ext, reach - distance), SEQ, -distance)
    grad_kv = summed_kv.astype(jnp.bfloat16)
    grad_act = jnp.concatenate([grad_q, grad_kv], axis=1)
    token_term = contract_cols(grad_act, proj_full).astype(jnp.bfloat16)
    n_tp = lax.psum(1, TP)
    cols = token_term.shape[1] // n_tp
    parts = lax.all_to_all(token_term.reshape(tok_rows, n_tp, cols), TP, 1, 1, tiled=True)
    grad_tokens = parts.astype(jnp.float32).sum(axis=1).astype(jnp.bfloat16)
    weight_terms = jnp.concatenate(
        [
            term_maker(full_tokens, grad_act).astype(jnp.bfloat16),
            term_maker(full_cot, attn).astype(jnp.bfloat16),
        ],
        axis=1,
    )
    summed = lax.psum_scatter(weight_terms, SEQ, scatter_dimension=0, tiled=True)
    grad_query = summed[:, :n_q]
    grad_key = summed[:, n_q : n_q + n_kv]
    grad_value = summed[:, n_q + n_kv : n_proj]
    grad_w_out = summed[:, n_proj:].T
    return (grad_tokens, grad_query, grad_key, grad_value, grad_w_out)


def solution(mesh):
    fine = Mesh(mesh.devices.reshape(SEQ_SPLIT + TP_SPLIT), SEQ + TP)
    in_specs = (
        P(SEQ, TP),
        P(SEQ, TP),
        P(SEQ, TP),
        P(SEQ, TP),
        P(TP, SEQ),
        P(SEQ, TP),
        P(SEQ, None),
    )
    out_specs = (P(SEQ, TP), P(SEQ, TP), P(SEQ, TP), P(SEQ, TP), P(TP, SEQ))
    return jax.shard_map(shards, mesh=fine, in_specs=in_specs, out_specs=out_specs, check_vma=False)
```

```python
import functools

import jax
import jax.numpy as jnp
from jax import lax
from jax.experimental import pallas as pl
from jax.sharding import Mesh
from jax.sharding import PartitionSpec as P

HEADS = 32
KV_HEADS = 16
HD = 128
WIN = 1024
ATTN_SCALAR = 168

SEQ = ("ylo", "x", "core")
TP = ("z", "yhi")
SEQ_SPLIT = (2, 4, 2)
TP_SPLIT = (8, 2)


def from_behind(block, axis, distance):
    devices = range(lax.psum(1, axis))
    route = [(i - distance, i) for i in devices if i - distance in devices]
    return lax.ppermute(block, axis, route)


def _nt(left, right):
    return lax.dot_general(left, right, (((1,), (1,)), ((), ())), preferred_element_type=jnp.float32)


def _nn(left, right):
    return lax.dot_general(left, right, (((1,), (0,)), ((), ())), preferred_element_type=jnp.float32)


def attention_kernel(q_ref, d_ref, kv_ref, lst_ref, attn_ref, gq_ref, dkv_ref, *, scale, block_len, span, head_dim):
    n_blocks = q_ref.shape[0] // block_len
    groups = q_ref.shape[1] // head_dim
    width = span * block_len
    dkv_ref[...] = jnp.zeros(dkv_ref.shape, jnp.float32)
    rows = lax.broadcasted_iota(jnp.int32, (block_len, width), 0)
    cols = lax.broadcasted_iota(jnp.int32, (block_len, width), 1)
    inside = (cols > rows) & (cols <= rows + (width - block_len))
    for b in range(n_blocks):
        w0 = b * block_len
        kw = kv_ref[w0 : w0 + width, :head_dim]
        vw = kv_ref[w0 : w0 + width, head_dim:]
        allowed = inside & (lst_ref[b : b + 1, :] > 0.0)
        dk_acc = jnp.zeros((width, head_dim), jnp.float32)
        dv_acc = jnp.zeros((width, head_dim), jnp.float32)
        for g in range(groups):
            r0, c0 = b * block_len, g * head_dim
            qb = q_ref[r0 : r0 + block_len, c0 : c0 + head_dim]
            db = d_ref[r0 : r0 + block_len, c0 : c0 + head_dim]
            scores = _nt(qb, kw) * scale
            masked = jnp.where(allowed, scores, -1e30)
            highest = jnp.max(masked, axis=1, keepdims=True)
            weights = jnp.where(allowed, jnp.exp(masked - highest), 0.0)
            probs = weights / jnp.sum(weights, axis=1, keepdims=True)
            probs_half = probs.astype(jnp.bfloat16)
            attn = _nn(probs_half, vw).astype(jnp.bfloat16)
            attn_ref[r0 : r0 + block_len, c0 : c0 + head_dim] = attn
            delta = jnp.sum(db.astype(jnp.float32) * attn.astype(jnp.float32), axis=1, keepdims=True)
            grad_probs = _nt(db, vw)
            grad_scores = (probs * (grad_probs - delta)).astype(jnp.bfloat16)
            grad_q = _nn(grad_scores, kw) * scale
            gq_ref[r0 : r0 + block_len, c0 : c0 + head_dim] = grad_q.astype(jnp.bfloat16)
            dk_acc = dk_acc + _nn(grad_scores.T, qb)
            dv_acc = dv_acc + _nn(probs_half.T, db)
        dkv_ref[w0 : w0 + width, :head_dim] += dk_acc * scale
        dkv_ref[w0 : w0 + width, head_dim:] += dv_acc


def fused_attention(query, kv_ext, d_attn, block_lists, scale, head_dim):
    n_blocks, span = block_lists.shape
    block_len = query.shape[0] // n_blocks
    listed = jnp.repeat((block_lists >= 0).astype(jnp.float32), block_len, axis=1)
    body = functools.partial(
        attention_kernel, scale=scale, block_len=block_len, span=span, head_dim=head_dim
    )
    return pl.pallas_call(
        body,
        out_shape=(
            jax.ShapeDtypeStruct(query.shape, jnp.bfloat16),
            jax.ShapeDtypeStruct(query.shape, jnp.bfloat16),
            jax.ShapeDtypeStruct(kv_ext.shape, jnp.float32),
        ),
    )(query, d_attn, kv_ext, listed)


def weight_terms_kernel(tok_ref, cot_ref, ga_ref, attn_ref, out_ref):
    n_act = ga_ref.shape[1]
    out_ref[:, :n_act] = _nn(tok_ref[...], ga_ref[...]).astype(out_ref.dtype)
    out_ref[:, n_act:] = _nn(cot_ref[...], attn_ref[...]).astype(out_ref.dtype)


def weight_terms(tokens_t, cot_t, grad_act, attn, block=768):
    feats, rows = tokens_t.shape
    n_act, n_attn = grad_act.shape[1], attn.shape[1]
    return pl.pallas_call(
        weight_terms_kernel,
        grid=(feats // block,),
        in_specs=[
            pl.BlockSpec((block, rows), lambda i: (i, 0)),
            pl.BlockSpec((block, rows), lambda i: (i, 0)),
            pl.BlockSpec((rows, n_act), lambda i: (0, 0)),
            pl.BlockSpec((rows, n_attn), lambda i: (0, 0)),
        ],
        out_specs=pl.BlockSpec((block, n_act + n_attn), lambda i: (i, 0)),
        out_shape=jax.ShapeDtypeStruct((feats, n_act + n_attn), jnp.bfloat16),
    )(tokens_t, cot_t, grad_act, attn)


def contract_cols(left, right):
    return lax.dot_general(
        left, right, (((1,), (1,)), ((), ())), preferred_element_type=jnp.float32
    )


def term_maker(left, right):
    return lax.dot_general(
        left, right, (((0,), (0,)), ((), ())), preferred_element_type=jnp.float32
    )


def shards(tokens, w_query, w_key, w_value, w_out, cotangent, block_lists):
    softmax_scale = ATTN_SCALAR ** (-0.5)
    head_dim = HD
    tok_rows = tokens.shape[0]
    reach = WIN // tok_rows
    n_q = w_query.shape[1]
    n_kv = w_key.shape[1]
    n_proj = n_q + 2 * n_kv
    pair = jnp.stack([tokens, cotangent])
    pair = lax.all_gather(pair, "yhi", axis=2, tiled=True)
    pair = lax.all_gather(pair, "z", axis=2, tiled=True)
    full_tokens, full_cot = pair[0], pair[1]
    w_cat = jnp.concatenate([w_query, w_key, w_value, w_out.T], axis=1)
    w_full = lax.all_gather(w_cat, SEQ, axis=0, tiled=True)
    proj_full = w_full[:, :n_proj]
    d_attn = jnp.dot(full_cot, w_full[:, n_proj:], preferred_element_type=jnp.float32).astype(
        jnp.bfloat16
    )
    qkv = jnp.dot(full_tokens, proj_full, preferred_element_type=jnp.float32).astype(jnp.bfloat16)
    query = qkv[:, :n_q]
    kv = qkv[:, n_q:]
    earlier = [from_behind(kv, SEQ, distance) for distance in range(reach, 0, -1)]
    kv_ext = jnp.concatenate(earlier + [kv], axis=0)
    attn, grad_q, grad_kv_ext = fused_attention(
        query, kv_ext, d_attn, block_lists, softmax_scale, head_dim
    )

    def segment(array, index):
        return array[index * tok_rows : (index + 1) * tok_rows]

    summed_kv = segment(grad_kv_ext, reach)
    for distance in range(1, reach + 1):
        summed_kv = summed_kv + from_behind(segment(grad_kv_ext, reach - distance), SEQ, -distance)
    grad_kv = summed_kv.astype(jnp.bfloat16)
    grad_act = jnp.concatenate([grad_q, grad_kv], axis=1)
    token_term = contract_cols(grad_act, proj_full).astype(jnp.bfloat16)
    n_tp = lax.psum(1, TP)
    cols = token_term.shape[1] // n_tp
    parts = lax.all_to_all(token_term.reshape(tok_rows, n_tp, cols), TP, 1, 1, tiled=True)
    grad_tokens = parts.astype(jnp.float32).sum(axis=1).astype(jnp.bfloat16)
    weight_parts = weight_terms(full_tokens.T, full_cot.T, grad_act, attn)
    summed = lax.psum_scatter(weight_parts, SEQ, scatter_dimension=0, tiled=True)
    grad_query = summed[:, :n_q]
    grad_key = summed[:, n_q : n_q + n_kv]
    grad_value = summed[:, n_q + n_kv : n_proj]
    grad_w_out = summed[:, n_proj:].T
    return (grad_tokens, grad_query, grad_key, grad_value, grad_w_out)


def solution(mesh):
    fine = Mesh(mesh.devices.reshape(SEQ_SPLIT + TP_SPLIT), SEQ + TP)
    in_specs = (
        P(SEQ, TP),
        P(SEQ, TP),
        P(SEQ, TP),
        P(SEQ, TP),
        P(TP, SEQ),
        P(SEQ, TP),
        P(SEQ, None),
    )
    out_specs = (P(SEQ, TP), P(SEQ, TP), P(SEQ, TP), P(SEQ, TP), P(TP, SEQ))
    return jax.shard_map(shards, mesh=fine, in_specs=in_specs, out_specs=out_specs, check_vma=False)
```

```python
import functools

import jax
import jax.numpy as jnp
from jax import lax
from jax.experimental import pallas as pl
from jax.sharding import Mesh
from jax.sharding import PartitionSpec as P

HEADS = 32
KV_HEADS = 16
HD = 128
WIN = 1024
ATTN_SCALAR = 168

SEQ = ("ylo", "x", "core")
TP = ("z", "yhi")
SEQ_SPLIT = (2, 4, 2)
TP_SPLIT = (8, 2)


def ring_gather(block, axis, dim):
    size = lax.psum(1, axis)
    right, left = [block], [block]
    for _ in range(size // 2):
        right.append(lax.ppermute(right[-1], axis, [(i, (i + 1) % size) for i in range(size)]))
    for _ in range((size - 1) // 2):
        left.append(lax.ppermute(left[-1], axis, [(i, (i - 1) % size) for i in range(size)]))
    ordered = left + [right[k] for k in range(size // 2, 0, -1)]
    relative = jnp.concatenate(ordered, axis=dim)
    return jnp.roll(relative, lax.axis_index(axis) * block.shape[dim], axis=dim)


def from_behind(block, axis, distance):
    devices = range(lax.psum(1, axis))
    route = [(i - distance, i) for i in devices if i - distance in devices]
    return lax.ppermute(block, axis, route)


def _nt(left, right):
    return lax.dot_general(left, right, (((1,), (1,)), ((), ())), preferred_element_type=jnp.float32)


def _nn(left, right):
    return lax.dot_general(left, right, (((1,), (0,)), ((), ())), preferred_element_type=jnp.float32)


def attention_kernel(q_ref, d_ref, kv_ref, lst_ref, attn_ref, gq_ref, dkv_ref, *, scale, block_len, span, head_dim):
    n_blocks = q_ref.shape[0] // block_len
    groups = q_ref.shape[1] // head_dim
    width = span * block_len
    dkv_ref[...] = jnp.zeros(dkv_ref.shape, jnp.float32)
    rows = lax.broadcasted_iota(jnp.int32, (block_len, width), 0)
    cols = lax.broadcasted_iota(jnp.int32, (block_len, width), 1)
    inside = (cols > rows) & (cols <= rows + (width - block_len))
    for b in range(n_blocks):
        w0 = b * block_len
        kw = kv_ref[w0 : w0 + width, :head_dim]
        vw = kv_ref[w0 : w0 + width, head_dim:]
        allowed = inside & (lst_ref[b : b + 1, :] > 0.0)
        dk_acc = jnp.zeros((width, head_dim), jnp.float32)
        dv_acc = jnp.zeros((width, head_dim), jnp.float32)
        for g in range(groups):
            r0, c0 = b * block_len, g * head_dim
            qb = q_ref[r0 : r0 + block_len, c0 : c0 + head_dim]
            db = d_ref[r0 : r0 + block_len, c0 : c0 + head_dim]
            scores = _nt(qb, kw) * scale
            masked = jnp.where(allowed, scores, -1e30)
            highest = jnp.max(masked, axis=1, keepdims=True)
            weights = jnp.where(allowed, jnp.exp(masked - highest), 0.0)
            probs = weights / jnp.sum(weights, axis=1, keepdims=True)
            probs_half = probs.astype(jnp.bfloat16)
            attn = _nn(probs_half, vw).astype(jnp.bfloat16)
            attn_ref[r0 : r0 + block_len, c0 : c0 + head_dim] = attn
            delta = jnp.sum(db.astype(jnp.float32) * attn.astype(jnp.float32), axis=1, keepdims=True)
            grad_probs = _nt(db, vw)
            grad_scores = (probs * (grad_probs - delta)).astype(jnp.bfloat16)
            grad_q = _nn(grad_scores, kw) * scale
            gq_ref[r0 : r0 + block_len, c0 : c0 + head_dim] = grad_q.astype(jnp.bfloat16)
            dk_acc = dk_acc + _nn(grad_scores.T, qb)
            dv_acc = dv_acc + _nn(probs_half.T, db)
        dkv_ref[w0 : w0 + width, :head_dim] += dk_acc * scale
        dkv_ref[w0 : w0 + width, head_dim:] += dv_acc


def fused_attention(query, kv_ext, d_attn, block_lists, scale, head_dim):
    n_blocks, span = block_lists.shape
    block_len = query.shape[0] // n_blocks
    listed = jnp.repeat((block_lists >= 0).astype(jnp.float32), block_len, axis=1)
    body = functools.partial(
        attention_kernel, scale=scale, block_len=block_len, span=span, head_dim=head_dim
    )
    return pl.pallas_call(
        body,
        out_shape=(
            jax.ShapeDtypeStruct(query.shape, jnp.bfloat16),
            jax.ShapeDtypeStruct(query.shape, jnp.bfloat16),
            jax.ShapeDtypeStruct(kv_ext.shape, jnp.float32),
        ),
    )(query, d_attn, kv_ext, listed)


def weight_terms_kernel(tok_ref, cot_ref, ga_ref, attn_ref, out_ref):
    n_act = ga_ref.shape[1]
    out_ref[:, :n_act] = _nn(tok_ref[...], ga_ref[...]).astype(out_ref.dtype)
    out_ref[:, n_act:] = _nn(cot_ref[...], attn_ref[...]).astype(out_ref.dtype)


def weight_terms(tokens_t, cot_t, grad_act, attn, block=768):
    feats, rows = tokens_t.shape
    n_act, n_attn = grad_act.shape[1], attn.shape[1]
    return pl.pallas_call(
        weight_terms_kernel,
        grid=(feats // block,),
        in_specs=[
            pl.BlockSpec((block, rows), lambda i: (i, 0)),
            pl.BlockSpec((block, rows), lambda i: (i, 0)),
            pl.BlockSpec((rows, n_act), lambda i: (0, 0)),
            pl.BlockSpec((rows, n_attn), lambda i: (0, 0)),
        ],
        out_specs=pl.BlockSpec((block, n_act + n_attn), lambda i: (i, 0)),
        out_shape=jax.ShapeDtypeStruct((feats, n_act + n_attn), jnp.bfloat16),
    )(tokens_t, cot_t, grad_act, attn)


def contract_cols(left, right):
    return lax.dot_general(
        left, right, (((1,), (1,)), ((), ())), preferred_element_type=jnp.float32
    )


def term_maker(left, right):
    return lax.dot_general(
        left, right, (((0,), (0,)), ((), ())), preferred_element_type=jnp.float32
    )


def shards(tokens, w_query, w_key, w_value, w_out, cotangent, block_lists):
    softmax_scale = ATTN_SCALAR ** (-0.5)
    head_dim = HD
    tok_rows = tokens.shape[0]
    reach = WIN // tok_rows
    n_q = w_query.shape[1]
    n_kv = w_key.shape[1]
    n_proj = n_q + 2 * n_kv
    pair = jnp.stack([tokens, cotangent])
    pair = lax.all_gather(pair, "yhi", axis=2, tiled=True)
    pair = ring_gather(pair, "z", 2)
    full_tokens, full_cot = pair[0], pair[1]
    w_cat = jnp.concatenate([w_query, w_key, w_value, w_out.T], axis=1)
    w_full = lax.all_gather(w_cat, SEQ, axis=0, tiled=True)
    proj_full = w_full[:, :n_proj]
    d_attn = jnp.dot(full_cot, w_full[:, n_proj:], preferred_element_type=jnp.float32).astype(
        jnp.bfloat16
    )
    qkv = jnp.dot(full_tokens, proj_full, preferred_element_type=jnp.float32).astype(jnp.bfloat16)
    query = qkv[:, :n_q]
    kv = qkv[:, n_q:]
    earlier = [from_behind(kv, SEQ, distance) for distance in range(reach, 0, -1)]
    kv_ext = jnp.concatenate(earlier + [kv], axis=0)
    attn, grad_q, grad_kv_ext = fused_attention(
        query, kv_ext, d_attn, block_lists, softmax_scale, head_dim
    )

    def segment(array, index):
        return array[index * tok_rows : (index + 1) * tok_rows]

    summed_kv = segment(grad_kv_ext, reach)
    for distance in range(1, reach + 1):
        summed_kv = summed_kv + from_behind(segment(grad_kv_ext, reach - distance), SEQ, -distance)
    grad_kv = summed_kv.astype(jnp.bfloat16)
    grad_act = jnp.concatenate([grad_q, grad_kv], axis=1)
    token_term = contract_cols(grad_act, proj_full).astype(jnp.bfloat16)
    n_tp = lax.psum(1, TP)
    cols = token_term.shape[1] // n_tp
    parts = lax.all_to_all(token_term.reshape(tok_rows, n_tp, cols), TP, 1, 1, tiled=True)
    grad_tokens = parts.astype(jnp.float32).sum(axis=1).astype(jnp.bfloat16)
    weight_parts = weight_terms(full_tokens.T, full_cot.T, grad_act, attn)
    summed = lax.psum_scatter(weight_parts, SEQ, scatter_dimension=0, tiled=True)
    grad_query = summed[:, :n_q]
    grad_key = summed[:, n_q : n_q + n_kv]
    grad_value = summed[:, n_q + n_kv : n_proj]
    grad_w_out = summed[:, n_proj:].T
    return (grad_tokens, grad_query, grad_key, grad_value, grad_w_out)


def solution(mesh):
    fine = Mesh(mesh.devices.reshape(SEQ_SPLIT + TP_SPLIT), SEQ + TP)
    in_specs = (
        P(SEQ, TP),
        P(SEQ, TP),
        P(SEQ, TP),
        P(SEQ, TP),
        P(TP, SEQ),
        P(SEQ, TP),
        P(SEQ, None),
    )
    out_specs = (P(SEQ, TP), P(SEQ, TP), P(SEQ, TP), P(SEQ, TP), P(TP, SEQ))
    return jax.shard_map(shards, mesh=fine, in_specs=in_specs, out_specs=out_specs, check_vma=False)
```

```python
import functools

import jax
import jax.numpy as jnp
from jax import lax
from jax.experimental import pallas as pl
from jax.sharding import Mesh
from jax.sharding import PartitionSpec as P

HEADS = 32
KV_HEADS = 16
HD = 128
WIN = 1024
ATTN_SCALAR = 168

SEQ = ("ylo", "x", "core")
TP = ("z", "yhi")
SEQ_SPLIT = (2, 4, 2)
TP_SPLIT = (8, 2)


def ring_gather(block, axis, dim):
    size = lax.psum(1, axis)
    index = lax.axis_index(axis)
    right, left = [block], [block]
    for _ in range(size // 2):
        right.append(lax.ppermute(right[-1], axis, [(i, (i + 1) % size) for i in range(size)]))
    for _ in range((size - 1) // 2):
        left.append(lax.ppermute(left[-1], axis, [(i, (i - 1) % size) for i in range(size)]))
    ordered = left + [right[k] for k in range(size // 2, 0, -1)]
    shape = list(block.shape)
    shape[dim] *= size
    full = jnp.zeros(shape, block.dtype)
    for offset, piece in enumerate(ordered):
        start = [0] * len(shape)
        start[dim] = ((index + offset) % size) * block.shape[dim]
        full = lax.dynamic_update_slice(full, piece, start)
    return full


def from_behind(block, axis, distance):
    devices = range(lax.psum(1, axis))
    route = [(i - distance, i) for i in devices if i - distance in devices]
    return lax.ppermute(block, axis, route)


def _nt(left, right):
    return lax.dot_general(left, right, (((1,), (1,)), ((), ())), preferred_element_type=jnp.float32)


def _nn(left, right):
    return lax.dot_general(left, right, (((1,), (0,)), ((), ())), preferred_element_type=jnp.float32)


def attention_kernel(q_ref, d_ref, kv_ref, lst_ref, attn_ref, gq_ref, dkv_ref, *, scale, block_len, span, head_dim):
    n_blocks = q_ref.shape[0] // block_len
    groups = q_ref.shape[1] // head_dim
    width = span * block_len
    dkv_ref[...] = jnp.zeros(dkv_ref.shape, jnp.float32)
    rows = lax.broadcasted_iota(jnp.int32, (block_len, width), 0)
    cols = lax.broadcasted_iota(jnp.int32, (block_len, width), 1)
    inside = (cols > rows) & (cols <= rows + (width - block_len))
    for b in range(n_blocks):
        w0 = b * block_len
        kw = kv_ref[w0 : w0 + width, :head_dim]
        vw = kv_ref[w0 : w0 + width, head_dim:]
        allowed = inside & (lst_ref[b : b + 1, :] > 0.0)
        dk_acc = jnp.zeros((width, head_dim), jnp.float32)
        dv_acc = jnp.zeros((width, head_dim), jnp.float32)
        for g in range(groups):
            r0, c0 = b * block_len, g * head_dim
            qb = q_ref[r0 : r0 + block_len, c0 : c0 + head_dim]
            db = d_ref[r0 : r0 + block_len, c0 : c0 + head_dim]
            scores = _nt(qb, kw) * scale
            masked = jnp.where(allowed, scores, -1e30)
            highest = jnp.max(masked, axis=1, keepdims=True)
            weights = jnp.where(allowed, jnp.exp(masked - highest), 0.0)
            probs = weights / jnp.sum(weights, axis=1, keepdims=True)
            probs_half = probs.astype(jnp.bfloat16)
            attn = _nn(probs_half, vw).astype(jnp.bfloat16)
            attn_ref[r0 : r0 + block_len, c0 : c0 + head_dim] = attn
            delta = jnp.sum(db.astype(jnp.float32) * attn.astype(jnp.float32), axis=1, keepdims=True)
            grad_probs = _nt(db, vw)
            grad_scores = (probs * (grad_probs - delta)).astype(jnp.bfloat16)
            grad_q = _nn(grad_scores, kw) * scale
            gq_ref[r0 : r0 + block_len, c0 : c0 + head_dim] = grad_q.astype(jnp.bfloat16)
            dk_acc = dk_acc + _nn(grad_scores.T, qb)
            dv_acc = dv_acc + _nn(probs_half.T, db)
        dkv_ref[w0 : w0 + width, :head_dim] += dk_acc * scale
        dkv_ref[w0 : w0 + width, head_dim:] += dv_acc


def fused_attention(query, kv_ext, d_attn, block_lists, scale, head_dim):
    n_blocks, span = block_lists.shape
    block_len = query.shape[0] // n_blocks
    listed = jnp.repeat((block_lists >= 0).astype(jnp.float32), block_len, axis=1)
    body = functools.partial(
        attention_kernel, scale=scale, block_len=block_len, span=span, head_dim=head_dim
    )
    return pl.pallas_call(
        body,
        out_shape=(
            jax.ShapeDtypeStruct(query.shape, jnp.bfloat16),
            jax.ShapeDtypeStruct(query.shape, jnp.bfloat16),
            jax.ShapeDtypeStruct(kv_ext.shape, jnp.float32),
        ),
    )(query, d_attn, kv_ext, listed)


def weight_terms_kernel(tok_ref, cot_ref, ga_ref, attn_ref, out_ref):
    n_act = ga_ref.shape[1]
    out_ref[:, :n_act] = _nn(tok_ref[...], ga_ref[...]).astype(out_ref.dtype)
    out_ref[:, n_act:] = _nn(cot_ref[...], attn_ref[...]).astype(out_ref.dtype)


def weight_terms(tokens_t, cot_t, grad_act, attn, block=768):
    feats, rows = tokens_t.shape
    n_act, n_attn = grad_act.shape[1], attn.shape[1]
    return pl.pallas_call(
        weight_terms_kernel,
        grid=(feats // block,),
        in_specs=[
            pl.BlockSpec((block, rows), lambda i: (i, 0)),
            pl.BlockSpec((block, rows), lambda i: (i, 0)),
            pl.BlockSpec((rows, n_act), lambda i: (0, 0)),
            pl.BlockSpec((rows, n_attn), lambda i: (0, 0)),
        ],
        out_specs=pl.BlockSpec((block, n_act + n_attn), lambda i: (i, 0)),
        out_shape=jax.ShapeDtypeStruct((feats, n_act + n_attn), jnp.bfloat16),
    )(tokens_t, cot_t, grad_act, attn)


def contract_cols(left, right):
    return lax.dot_general(
        left, right, (((1,), (1,)), ((), ())), preferred_element_type=jnp.float32
    )


def term_maker(left, right):
    return lax.dot_general(
        left, right, (((0,), (0,)), ((), ())), preferred_element_type=jnp.float32
    )


def shards(tokens, w_query, w_key, w_value, w_out, cotangent, block_lists):
    softmax_scale = ATTN_SCALAR ** (-0.5)
    head_dim = HD
    tok_rows = tokens.shape[0]
    reach = WIN // tok_rows
    n_q = w_query.shape[1]
    n_kv = w_key.shape[1]
    n_proj = n_q + 2 * n_kv
    pair = jnp.stack([tokens, cotangent])
    pair = lax.all_gather(pair, "yhi", axis=2, tiled=True)
    full_tokens = ring_gather(pair[0], "z", 1)
    full_cot = lax.all_gather(pair[1], "z", axis=1, tiled=True)
    w_cat = jnp.concatenate([w_query, w_key, w_value, w_out.T], axis=1)
    w_full = lax.all_gather(w_cat, SEQ, axis=0, tiled=True)
    proj_full = w_full[:, :n_proj]
    d_attn = jnp.dot(full_cot, w_full[:, n_proj:], preferred_element_type=jnp.float32).astype(
        jnp.bfloat16
    )
    qkv = jnp.dot(full_tokens, proj_full, preferred_element_type=jnp.float32).astype(jnp.bfloat16)
    query = qkv[:, :n_q]
    kv = qkv[:, n_q:]
    earlier = [from_behind(kv, SEQ, distance) for distance in range(reach, 0, -1)]
    kv_ext = jnp.concatenate(earlier + [kv], axis=0)
    attn, grad_q, grad_kv_ext = fused_attention(
        query, kv_ext, d_attn, block_lists, softmax_scale, head_dim
    )

    def segment(array, index):
        return array[index * tok_rows : (index + 1) * tok_rows]

    summed_kv = segment(grad_kv_ext, reach)
    for distance in range(1, reach + 1):
        summed_kv = summed_kv + from_behind(segment(grad_kv_ext, reach - distance), SEQ, -distance)
    grad_kv = summed_kv.astype(jnp.bfloat16)
    grad_act = jnp.concatenate([grad_q, grad_kv], axis=1)
    token_term = contract_cols(grad_act, proj_full).astype(jnp.bfloat16)
    n_tp = lax.psum(1, TP)
    cols = token_term.shape[1] // n_tp
    parts = lax.all_to_all(token_term.reshape(tok_rows, n_tp, cols), TP, 1, 1, tiled=True)
    grad_tokens = parts.astype(jnp.float32).sum(axis=1).astype(jnp.bfloat16)
    weight_parts = weight_terms(full_tokens.T, full_cot.T, grad_act, attn)
    summed = lax.psum_scatter(weight_parts, SEQ, scatter_dimension=0, tiled=True)
    grad_query = summed[:, :n_q]
    grad_key = summed[:, n_q : n_q + n_kv]
    grad_value = summed[:, n_q + n_kv : n_proj]
    grad_w_out = summed[:, n_proj:].T
    return (grad_tokens, grad_query, grad_key, grad_value, grad_w_out)


def solution(mesh):
    fine = Mesh(mesh.devices.reshape(SEQ_SPLIT + TP_SPLIT), SEQ + TP)
    in_specs = (
        P(SEQ, TP),
        P(SEQ, TP),
        P(SEQ, TP),
        P(SEQ, TP),
        P(TP, SEQ),
        P(SEQ, TP),
        P(SEQ, None),
    )
    out_specs = (P(SEQ, TP), P(SEQ, TP), P(SEQ, TP), P(SEQ, TP), P(TP, SEQ))
    return jax.shard_map(shards, mesh=fine, in_specs=in_specs, out_specs=out_specs, check_vma=False)
```

```python
import functools

import jax
import jax.numpy as jnp
from jax import lax
from jax.experimental import pallas as pl
from jax.sharding import Mesh
from jax.sharding import PartitionSpec as P

HEADS = 32
KV_HEADS = 16
HD = 128
WIN = 1024
ATTN_SCALAR = 168

SEQ = ("ylo", "x", "core")
TP = ("z", "yhi")
SEQ_SPLIT = (2, 4, 2)
TP_SPLIT = (8, 2)


def ring_gather(block, axis, dim):
    size = lax.psum(1, axis)
    index = lax.axis_index(axis)
    right, left = [block], [block]
    for _ in range(size // 2):
        right.append(lax.ppermute(right[-1], axis, [(i, (i + 1) % size) for i in range(size)]))
    for _ in range((size - 1) // 2):
        left.append(lax.ppermute(left[-1], axis, [(i, (i - 1) % size) for i in range(size)]))
    ordered = left + [right[k] for k in range(size // 2, 0, -1)]
    shape = list(block.shape)
    shape[dim] *= size
    full = jnp.zeros(shape, block.dtype)
    for offset, piece in enumerate(ordered):
        start = [0] * len(shape)
        start[dim] = ((index + offset) % size) * block.shape[dim]
        full = lax.dynamic_update_slice(full, piece, start)
    return full


def from_behind(block, axis, distance):
    devices = range(lax.psum(1, axis))
    route = [(i - distance, i) for i in devices if i - distance in devices]
    return lax.ppermute(block, axis, route)


def _nt(left, right):
    return lax.dot_general(left, right, (((1,), (1,)), ((), ())), preferred_element_type=jnp.float32)


def _nn(left, right):
    return lax.dot_general(left, right, (((1,), (0,)), ((), ())), preferred_element_type=jnp.float32)


def attention_kernel(q_ref, d_ref, kv_ref, lst_ref, attn_ref, gq_ref, dkv_ref, *, scale, block_len, span, head_dim):
    n_blocks = q_ref.shape[0] // block_len
    groups = q_ref.shape[1] // head_dim
    width = span * block_len
    dkv_ref[...] = jnp.zeros(dkv_ref.shape, jnp.float32)
    rows = lax.broadcasted_iota(jnp.int32, (block_len, width), 0)
    cols = lax.broadcasted_iota(jnp.int32, (block_len, width), 1)
    inside = (cols > rows) & (cols <= rows + (width - block_len))
    for b in range(n_blocks):
        w0 = b * block_len
        kw = kv_ref[w0 : w0 + width, :head_dim]
        vw = kv_ref[w0 : w0 + width, head_dim:]
        allowed = inside & (lst_ref[b : b + 1, :] > 0.0)
        dk_acc = jnp.zeros((width, head_dim), jnp.float32)
        dv_acc = jnp.zeros((width, head_dim), jnp.float32)
        for g in range(groups):
            r0, c0 = b * block_len, g * head_dim
            qb = q_ref[r0 : r0 + block_len, c0 : c0 + head_dim]
            db = d_ref[r0 : r0 + block_len, c0 : c0 + head_dim]
            scores = _nt(qb, kw) * scale
            masked = jnp.where(allowed, scores, -1e30)
            highest = jnp.max(masked, axis=1, keepdims=True)
            weights = jnp.where(allowed, jnp.exp(masked - highest), 0.0)
            probs = weights / jnp.sum(weights, axis=1, keepdims=True)
            probs_half = probs.astype(jnp.bfloat16)
            attn = _nn(probs_half, vw).astype(jnp.bfloat16)
            attn_ref[r0 : r0 + block_len, c0 : c0 + head_dim] = attn
            delta = jnp.sum(db.astype(jnp.float32) * attn.astype(jnp.float32), axis=1, keepdims=True)
            grad_probs = _nt(db, vw)
            grad_scores = (probs * (grad_probs - delta)).astype(jnp.bfloat16)
            grad_q = _nn(grad_scores, kw) * scale
            gq_ref[r0 : r0 + block_len, c0 : c0 + head_dim] = grad_q.astype(jnp.bfloat16)
            dk_acc = dk_acc + _nn(grad_scores.T, qb)
            dv_acc = dv_acc + _nn(probs_half.T, db)
        dkv_ref[w0 : w0 + width, :head_dim] += dk_acc * scale
        dkv_ref[w0 : w0 + width, head_dim:] += dv_acc


def fused_attention(query, kv_ext, d_attn, block_lists, scale, head_dim):
    n_blocks, span = block_lists.shape
    block_len = query.shape[0] // n_blocks
    listed = jnp.repeat((block_lists >= 0).astype(jnp.float32), block_len, axis=1)
    body = functools.partial(
        attention_kernel, scale=scale, block_len=block_len, span=span, head_dim=head_dim
    )
    return pl.pallas_call(
        body,
        out_shape=(
            jax.ShapeDtypeStruct(query.shape, jnp.bfloat16),
            jax.ShapeDtypeStruct(query.shape, jnp.bfloat16),
            jax.ShapeDtypeStruct(kv_ext.shape, jnp.float32),
        ),
    )(query, d_attn, kv_ext, listed)


def weight_terms_kernel(tok_ref, cot_ref, ga_ref, attn_ref, out_ref):
    n_act = ga_ref.shape[1]
    out_ref[:, :n_act] = _nn(tok_ref[...], ga_ref[...]).astype(out_ref.dtype)
    out_ref[:, n_act:] = _nn(cot_ref[...], attn_ref[...]).astype(out_ref.dtype)


def weight_terms(tokens_t, cot_t, grad_act, attn, block=768):
    feats, rows = tokens_t.shape
    n_act, n_attn = grad_act.shape[1], attn.shape[1]
    return pl.pallas_call(
        weight_terms_kernel,
        grid=(feats // block,),
        in_specs=[
            pl.BlockSpec((block, rows), lambda i: (i, 0)),
            pl.BlockSpec((block, rows), lambda i: (i, 0)),
            pl.BlockSpec((rows, n_act), lambda i: (0, 0)),
            pl.BlockSpec((rows, n_attn), lambda i: (0, 0)),
        ],
        out_specs=pl.BlockSpec((block, n_act + n_attn), lambda i: (i, 0)),
        out_shape=jax.ShapeDtypeStruct((feats, n_act + n_attn), jnp.bfloat16),
    )(tokens_t, cot_t, grad_act, attn)


def contract_cols(left, right):
    return lax.dot_general(
        left, right, (((1,), (1,)), ((), ())), preferred_element_type=jnp.float32
    )


def term_maker(left, right):
    return lax.dot_general(
        left, right, (((0,), (0,)), ((), ())), preferred_element_type=jnp.float32
    )


def shards(tokens, w_query, w_key, w_value, w_out, cotangent, block_lists):
    softmax_scale = ATTN_SCALAR ** (-0.5)
    head_dim = HD
    tok_rows = tokens.shape[0]
    reach = WIN // tok_rows
    n_q = w_query.shape[1]
    n_kv = w_key.shape[1]
    n_proj = n_q + 2 * n_kv
    pair = jnp.stack([tokens, cotangent])
    pair = lax.all_gather(pair, "yhi", axis=2, tiled=True)
    half = tok_rows // 2
    ring_full = ring_gather(jnp.concatenate([pair[0], pair[1][:half]], axis=0), "z", 1)
    full_tokens = ring_full[:tok_rows]
    cot_rest = lax.all_gather(pair[1][half:], "z", axis=1, tiled=True)
    full_cot = jnp.concatenate([ring_full[tok_rows:], cot_rest], axis=0)
    w_cat = jnp.concatenate([w_query, w_key, w_value, w_out.T], axis=1)
    w_full = lax.all_gather(w_cat, SEQ, axis=0, tiled=True)
    proj_full = w_full[:, :n_proj]
    d_attn = jnp.dot(full_cot, w_full[:, n_proj:], preferred_element_type=jnp.float32).astype(
        jnp.bfloat16
    )
    qkv = jnp.dot(full_tokens, proj_full, preferred_element_type=jnp.float32).astype(jnp.bfloat16)
    query = qkv[:, :n_q]
    kv = qkv[:, n_q:]
    earlier = [from_behind(kv, SEQ, distance) for distance in range(reach, 0, -1)]
    kv_ext = jnp.concatenate(earlier + [kv], axis=0)
    attn, grad_q, grad_kv_ext = fused_attention(
        query, kv_ext, d_attn, block_lists, softmax_scale, head_dim
    )

    def segment(array, index):
        return array[index * tok_rows : (index + 1) * tok_rows]

    summed_kv = segment(grad_kv_ext, reach)
    for distance in range(1, reach + 1):
        summed_kv = summed_kv + from_behind(segment(grad_kv_ext, reach - distance), SEQ, -distance)
    grad_kv = summed_kv.astype(jnp.bfloat16)
    grad_act = jnp.concatenate([grad_q, grad_kv], axis=1)
    token_term = contract_cols(grad_act, proj_full).astype(jnp.bfloat16)
    n_tp = lax.psum(1, TP)
    cols = token_term.shape[1] // n_tp
    parts = lax.all_to_all(token_term.reshape(tok_rows, n_tp, cols), TP, 1, 1, tiled=True)
    grad_tokens = parts.astype(jnp.float32).sum(axis=1).astype(jnp.bfloat16)
    weight_parts = weight_terms(full_tokens.T, full_cot.T, grad_act, attn)
    summed = lax.psum_scatter(weight_parts, SEQ, scatter_dimension=0, tiled=True)
    grad_query = summed[:, :n_q]
    grad_key = summed[:, n_q : n_q + n_kv]
    grad_value = summed[:, n_q + n_kv : n_proj]
    grad_w_out = summed[:, n_proj:].T
    return (grad_tokens, grad_query, grad_key, grad_value, grad_w_out)


def solution(mesh):
    fine = Mesh(mesh.devices.reshape(SEQ_SPLIT + TP_SPLIT), SEQ + TP)
    in_specs = (
        P(SEQ, TP),
        P(SEQ, TP),
        P(SEQ, TP),
        P(SEQ, TP),
        P(TP, SEQ),
        P(SEQ, TP),
        P(SEQ, None),
    )
    out_specs = (P(SEQ, TP), P(SEQ, TP), P(SEQ, TP), P(SEQ, TP), P(TP, SEQ))
    return jax.shard_map(shards, mesh=fine, in_specs=in_specs, out_specs=out_specs, check_vma=False)
```

```python
import functools

import jax
import jax.numpy as jnp
from jax import lax
from jax.experimental import pallas as pl
from jax.sharding import Mesh
from jax.sharding import PartitionSpec as P

HEADS = 32
KV_HEADS = 16
HD = 128
WIN = 1024
ATTN_SCALAR = 168

SEQ = ("ylo", "x", "core")
TP = ("z", "yhi")
SEQ_SPLIT = (2, 4, 2)
TP_SPLIT = (8, 2)


def ring_pieces(block, axis, dim):
    size = lax.psum(1, axis)
    index = lax.axis_index(axis)
    right, left = [block], [block]
    for _ in range(size // 2):
        right.append(lax.ppermute(right[-1], axis, [(i, (i + 1) % size) for i in range(size)]))
    for _ in range((size - 1) // 2):
        left.append(lax.ppermute(left[-1], axis, [(i, (i - 1) % size) for i in range(size)]))
    ordered = left + [right[k] for k in range(size // 2, 0, -1)]
    return [(((index + offset) % size) * block.shape[dim], piece) for offset, piece in enumerate(ordered)]


def place(pieces, dim, extent):
    shape = list(pieces[0][1].shape)
    shape[dim] = extent
    full = jnp.zeros(shape, pieces[0][1].dtype)
    for at, piece in pieces:
        start = [0] * len(shape)
        start[dim] = at
        full = lax.dynamic_update_slice(full, piece, start)
    return full


def piecewise_dot(pieces, weights):
    total = None
    for at, piece in pieces:
        rows = lax.dynamic_slice_in_dim(weights, at, piece.shape[1], axis=0)
        term = jnp.dot(piece, rows, preferred_element_type=jnp.float32)
        total = term if total is None else total + term
    return total.astype(jnp.bfloat16)


def from_behind(block, axis, distance):
    devices = range(lax.psum(1, axis))
    route = [(i - distance, i) for i in devices if i - distance in devices]
    return lax.ppermute(block, axis, route)


def _nt(left, right):
    return lax.dot_general(left, right, (((1,), (1,)), ((), ())), preferred_element_type=jnp.float32)


def _nn(left, right):
    return lax.dot_general(left, right, (((1,), (0,)), ((), ())), preferred_element_type=jnp.float32)


def attention_kernel(q_ref, d_ref, kv_ref, lst_ref, attn_ref, gq_ref, dkv_ref, *, scale, block_len, span, head_dim):
    n_blocks = q_ref.shape[0] // block_len
    groups = q_ref.shape[1] // head_dim
    width = span * block_len
    dkv_ref[...] = jnp.zeros(dkv_ref.shape, jnp.float32)
    rows = lax.broadcasted_iota(jnp.int32, (block_len, width), 0)
    cols = lax.broadcasted_iota(jnp.int32, (block_len, width), 1)
    inside = (cols > rows) & (cols <= rows + (width - block_len))
    for b in range(n_blocks):
        w0 = b * block_len
        kw = kv_ref[w0 : w0 + width, :head_dim]
        vw = kv_ref[w0 : w0 + width, head_dim:]
        allowed = inside & (lst_ref[b : b + 1, :] > 0.0)
        dk_acc = jnp.zeros((width, head_dim), jnp.float32)
        dv_acc = jnp.zeros((width, head_dim), jnp.float32)
        for g in range(groups):
            r0, c0 = b * block_len, g * head_dim
            qb = q_ref[r0 : r0 + block_len, c0 : c0 + head_dim]
            db = d_ref[r0 : r0 + block_len, c0 : c0 + head_dim]
            scores = _nt(qb, kw) * scale
            masked = jnp.where(allowed, scores, -1e30)
            highest = jnp.max(masked, axis=1, keepdims=True)
            weights = jnp.where(allowed, jnp.exp(masked - highest), 0.0)
            probs = weights / jnp.sum(weights, axis=1, keepdims=True)
            probs_half = probs.astype(jnp.bfloat16)
            attn = _nn(probs_half, vw).astype(jnp.bfloat16)
            attn_ref[r0 : r0 + block_len, c0 : c0 + head_dim] = attn
            delta = jnp.sum(db.astype(jnp.float32) * attn.astype(jnp.float32), axis=1, keepdims=True)
            grad_probs = _nt(db, vw)
            grad_scores = (probs * (grad_probs - delta)).astype(jnp.bfloat16)
            grad_q = _nn(grad_scores, kw) * scale
            gq_ref[r0 : r0 + block_len, c0 : c0 + head_dim] = grad_q.astype(jnp.bfloat16)
            dk_acc = dk_acc + _nn(grad_scores.T, qb)
            dv_acc = dv_acc + _nn(probs_half.T, db)
        dkv_ref[w0 : w0 + width, :head_dim] += dk_acc * scale
        dkv_ref[w0 : w0 + width, head_dim:] += dv_acc


def fused_attention(query, kv_ext, d_attn, block_lists, scale, head_dim):
    n_blocks, span = block_lists.shape
    block_len = query.shape[0] // n_blocks
    listed = jnp.repeat((block_lists >= 0).astype(jnp.float32), block_len, axis=1)
    body = functools.partial(
        attention_kernel, scale=scale, block_len=block_len, span=span, head_dim=head_dim
    )
    return pl.pallas_call(
        body,
        out_shape=(
            jax.ShapeDtypeStruct(query.shape, jnp.bfloat16),
            jax.ShapeDtypeStruct(query.shape, jnp.bfloat16),
            jax.ShapeDtypeStruct(kv_ext.shape, jnp.float32),
        ),
    )(query, d_attn, kv_ext, listed)


def weight_terms_kernel(tok_ref, cot_ref, ga_ref, attn_ref, out_ref):
    n_act = ga_ref.shape[1]
    out_ref[:, :n_act] = _nn(tok_ref[...], ga_ref[...]).astype(out_ref.dtype)
    out_ref[:, n_act:] = _nn(cot_ref[...], attn_ref[...]).astype(out_ref.dtype)


def weight_terms(tokens_t, cot_t, grad_act, attn, block=768):
    feats, rows = tokens_t.shape
    n_act, n_attn = grad_act.shape[1], attn.shape[1]
    return pl.pallas_call(
        weight_terms_kernel,
        grid=(feats // block,),
        in_specs=[
            pl.BlockSpec((block, rows), lambda i: (i, 0)),
            pl.BlockSpec((block, rows), lambda i: (i, 0)),
            pl.BlockSpec((rows, n_act), lambda i: (0, 0)),
            pl.BlockSpec((rows, n_attn), lambda i: (0, 0)),
        ],
        out_specs=pl.BlockSpec((block, n_act + n_attn), lambda i: (i, 0)),
        out_shape=jax.ShapeDtypeStruct((feats, n_act + n_attn), jnp.bfloat16),
    )(tokens_t, cot_t, grad_act, attn)


def contract_cols(left, right):
    return lax.dot_general(
        left, right, (((1,), (1,)), ((), ())), preferred_element_type=jnp.float32
    )


def term_maker(left, right):
    return lax.dot_general(
        left, right, (((0,), (0,)), ((), ())), preferred_element_type=jnp.float32
    )


def shards(tokens, w_query, w_key, w_value, w_out, cotangent, block_lists):
    softmax_scale = ATTN_SCALAR ** (-0.5)
    head_dim = HD
    tok_rows = tokens.shape[0]
    reach = WIN // tok_rows
    n_q = w_query.shape[1]
    n_kv = w_key.shape[1]
    n_proj = n_q + 2 * n_kv
    pair = jnp.stack([tokens, cotangent])
    pair = lax.all_gather(pair, "yhi", axis=2, tiled=True)
    pieces = ring_pieces(pair, "z", 2)
    feats = pair.shape[2] * len(pieces)
    tok_pieces = [(at, piece[0]) for at, piece in pieces]
    cot_pieces = [(at, piece[1]) for at, piece in pieces]
    full_tokens = place(tok_pieces, 1, feats)
    full_cot = place(cot_pieces, 1, feats)
    w_cat = jnp.concatenate([w_query, w_key, w_value, w_out.T], axis=1)
    w_full = lax.all_gather(w_cat, SEQ, axis=0, tiled=True)
    proj_full = w_full[:, :n_proj]
    d_attn = piecewise_dot(cot_pieces, w_full[:, n_proj:])
    qkv = piecewise_dot(tok_pieces, proj_full)
    query = qkv[:, :n_q]
    kv = qkv[:, n_q:]
    earlier = [from_behind(kv, SEQ, distance) for distance in range(reach, 0, -1)]
    kv_ext = jnp.concatenate(earlier + [kv], axis=0)
    attn, grad_q, grad_kv_ext = fused_attention(
        query, kv_ext, d_attn, block_lists, softmax_scale, head_dim
    )

    def segment(array, index):
        return array[index * tok_rows : (index + 1) * tok_rows]

    summed_kv = segment(grad_kv_ext, reach)
    for distance in range(1, reach + 1):
        summed_kv = summed_kv + from_behind(segment(grad_kv_ext, reach - distance), SEQ, -distance)
    grad_kv = summed_kv.astype(jnp.bfloat16)
    grad_act = jnp.concatenate([grad_q, grad_kv], axis=1)
    token_term = contract_cols(grad_act, proj_full).astype(jnp.bfloat16)
    n_tp = lax.psum(1, TP)
    cols = token_term.shape[1] // n_tp
    parts = lax.all_to_all(token_term.reshape(tok_rows, n_tp, cols), TP, 1, 1, tiled=True)
    grad_tokens = parts.astype(jnp.float32).sum(axis=1).astype(jnp.bfloat16)
    weight_parts = weight_terms(full_tokens.T, full_cot.T, grad_act, attn)
    summed = lax.psum_scatter(weight_parts, SEQ, scatter_dimension=0, tiled=True)
    grad_query = summed[:, :n_q]
    grad_key = summed[:, n_q : n_q + n_kv]
    grad_value = summed[:, n_q + n_kv : n_proj]
    grad_w_out = summed[:, n_proj:].T
    return (grad_tokens, grad_query, grad_key, grad_value, grad_w_out)


def solution(mesh):
    fine = Mesh(mesh.devices.reshape(SEQ_SPLIT + TP_SPLIT), SEQ + TP)
    in_specs = (
        P(SEQ, TP),
        P(SEQ, TP),
        P(SEQ, TP),
        P(SEQ, TP),
        P(TP, SEQ),
        P(SEQ, TP),
        P(SEQ, None),
    )
    out_specs = (P(SEQ, TP), P(SEQ, TP), P(SEQ, TP), P(SEQ, TP), P(TP, SEQ))
    return jax.shard_map(shards, mesh=fine, in_specs=in_specs, out_specs=out_specs, check_vma=False)
```

```python
import functools

import jax
import jax.numpy as jnp
from jax import lax
from jax.experimental import pallas as pl
from jax.sharding import Mesh
from jax.sharding import PartitionSpec as P

HEADS = 32
KV_HEADS = 16
HD = 128
WIN = 1024
ATTN_SCALAR = 168

SEQ = ("ylo", "x", "core")
TP = ("z", "yhi")
SEQ_SPLIT = (2, 4, 2)
TP_SPLIT = (8, 2)


def ring_gather(block, axis, dim):
    size = lax.psum(1, axis)
    index = lax.axis_index(axis)
    right, left = [block], [block]
    for _ in range(size // 2):
        right.append(lax.ppermute(right[-1], axis, [(i, (i + 1) % size) for i in range(size)]))
    for _ in range((size - 1) // 2):
        left.append(lax.ppermute(left[-1], axis, [(i, (i - 1) % size) for i in range(size)]))
    ordered = left + [right[k] for k in range(size // 2, 0, -1)]
    shape = list(block.shape)
    shape[dim] *= size
    full = jnp.zeros(shape, block.dtype)
    for offset, piece in enumerate(ordered):
        start = [0] * len(shape)
        start[dim] = ((index + offset) % size) * block.shape[dim]
        full = lax.dynamic_update_slice(full, piece, start)
    return full


def from_behind(block, axis, distance):
    devices = range(lax.psum(1, axis))
    route = [(i - distance, i) for i in devices if i - distance in devices]
    return lax.ppermute(block, axis, route)


def _nt(left, right):
    return lax.dot_general(left, right, (((1,), (1,)), ((), ())), preferred_element_type=jnp.float32)


def _nn(left, right):
    return lax.dot_general(left, right, (((1,), (0,)), ((), ())), preferred_element_type=jnp.float32)


def attention_kernel(q_ref, d_ref, kv_ref, lst_ref, attn_ref, gq_ref, dkv_ref, *, scale, block_len, span, head_dim):
    n_blocks = q_ref.shape[0] // block_len
    groups = q_ref.shape[1] // head_dim
    width = span * block_len
    dkv_ref[...] = jnp.zeros(dkv_ref.shape, jnp.float32)
    rows = lax.broadcasted_iota(jnp.int32, (block_len, width), 0)
    cols = lax.broadcasted_iota(jnp.int32, (block_len, width), 1)
    inside = (cols > rows) & (cols <= rows + (width - block_len))
    for b in range(n_blocks):
        w0 = b * block_len
        kw = kv_ref[w0 : w0 + width, :head_dim]
        vw = kv_ref[w0 : w0 + width, head_dim:]
        allowed = inside & (lst_ref[b : b + 1, :] > 0.0)
        dk_acc = jnp.zeros((width, head_dim), jnp.float32)
        dv_acc = jnp.zeros((width, head_dim), jnp.float32)
        for g in range(groups):
            r0, c0 = b * block_len, g * head_dim
            qb = q_ref[r0 : r0 + block_len, c0 : c0 + head_dim]
            db = d_ref[r0 : r0 + block_len, c0 : c0 + head_dim]
            scores = _nt(qb, kw) * scale
            masked = jnp.where(allowed, scores, -1e30)
            highest = jnp.max(masked, axis=1, keepdims=True)
            weights = jnp.where(allowed, jnp.exp(masked - highest), 0.0)
            probs = weights / jnp.sum(weights, axis=1, keepdims=True)
            probs_half = probs.astype(jnp.bfloat16)
            attn = _nn(probs_half, vw).astype(jnp.bfloat16)
            attn_ref[r0 : r0 + block_len, c0 : c0 + head_dim] = attn
            delta = jnp.sum(db.astype(jnp.float32) * attn.astype(jnp.float32), axis=1, keepdims=True)
            grad_probs = _nt(db, vw)
            grad_scores = (probs * (grad_probs - delta)).astype(jnp.bfloat16)
            grad_q = _nn(grad_scores, kw) * scale
            gq_ref[r0 : r0 + block_len, c0 : c0 + head_dim] = grad_q.astype(jnp.bfloat16)
            dk_acc = dk_acc + _nn(grad_scores.T, qb)
            dv_acc = dv_acc + _nn(probs_half.T, db)
        dkv_ref[w0 : w0 + width, :head_dim] += dk_acc * scale
        dkv_ref[w0 : w0 + width, head_dim:] += dv_acc


def fused_attention(query, kv_ext, d_attn, block_lists, scale, head_dim):
    n_blocks, span = block_lists.shape
    block_len = query.shape[0] // n_blocks
    listed = jnp.repeat((block_lists >= 0).astype(jnp.float32), block_len, axis=1)
    body = functools.partial(
        attention_kernel, scale=scale, block_len=block_len, span=span, head_dim=head_dim
    )
    return pl.pallas_call(
        body,
        out_shape=(
            jax.ShapeDtypeStruct(query.shape, jnp.bfloat16),
            jax.ShapeDtypeStruct(query.shape, jnp.bfloat16),
            jax.ShapeDtypeStruct(kv_ext.shape, jnp.float32),
        ),
    )(query, d_attn, kv_ext, listed)


def weight_terms_kernel(tok_ref, cot_ref, gq_ref, attn_ref, out_ref):
    n_q = gq_ref.shape[1]
    n_attn = attn_ref.shape[1]
    width = out_ref.shape[1]
    out_ref[:, :n_q] = _nn(tok_ref[...], gq_ref[...]).astype(out_ref.dtype)
    out_ref[:, n_q : width - n_attn] = jnp.zeros((out_ref.shape[0], width - n_attn - n_q), out_ref.dtype)
    out_ref[:, width - n_attn :] = _nn(cot_ref[...], attn_ref[...]).astype(out_ref.dtype)


def kv_terms_kernel(tok_ref, gkv_ref, base_ref, out_ref):
    del base_ref
    out_ref[...] = _nn(tok_ref[...], gkv_ref[...]).astype(out_ref.dtype)


def weight_terms(tokens_t, cot_t, grad_q, grad_kv, attn, block=768):
    feats, rows = tokens_t.shape
    n_q, n_kv, n_attn = grad_q.shape[1], grad_kv.shape[1], attn.shape[1]
    width = n_q + n_kv + n_attn
    first = pl.pallas_call(
        weight_terms_kernel,
        grid=(feats // block,),
        in_specs=[
            pl.BlockSpec((block, rows), lambda i: (i, 0)),
            pl.BlockSpec((block, rows), lambda i: (i, 0)),
            pl.BlockSpec((rows, n_q), lambda i: (0, 0)),
            pl.BlockSpec((rows, n_attn), lambda i: (0, 0)),
        ],
        out_specs=pl.BlockSpec((block, width), lambda i: (i, 0)),
        out_shape=jax.ShapeDtypeStruct((feats, width), jnp.bfloat16),
    )(tokens_t, cot_t, grad_q, attn)
    column = n_q // n_kv
    return pl.pallas_call(
        kv_terms_kernel,
        grid=(feats // block,),
        in_specs=[
            pl.BlockSpec((block, rows), lambda i: (i, 0)),
            pl.BlockSpec((rows, n_kv), lambda i: (0, 0)),
            pl.BlockSpec(memory_space=pl.ANY),
        ],
        out_specs=pl.BlockSpec((block, n_kv), lambda i: (i, column)),
        out_shape=jax.ShapeDtypeStruct((feats, width), jnp.bfloat16),
        input_output_aliases={2: 0},
    )(tokens_t, grad_kv, first)


def contract_cols(left, right):
    return lax.dot_general(
        left, right, (((1,), (1,)), ((), ())), preferred_element_type=jnp.float32
    )


def term_maker(left, right):
    return lax.dot_general(
        left, right, (((0,), (0,)), ((), ())), preferred_element_type=jnp.float32
    )


def shards(tokens, w_query, w_key, w_value, w_out, cotangent, block_lists):
    softmax_scale = ATTN_SCALAR ** (-0.5)
    head_dim = HD
    tok_rows = tokens.shape[0]
    reach = WIN // tok_rows
    n_q = w_query.shape[1]
    n_kv = w_key.shape[1]
    n_proj = n_q + 2 * n_kv
    pair = jnp.stack([tokens, cotangent])
    pair = lax.all_gather(pair, "yhi", axis=2, tiled=True)
    full_tokens = ring_gather(pair[0], "z", 1)
    full_cot = lax.all_gather(pair[1], "z", axis=1, tiled=True)
    w_cat = jnp.concatenate([w_query, w_key, w_value, w_out.T], axis=1)
    w_full = lax.all_gather(w_cat, SEQ, axis=0, tiled=True)
    proj_full = w_full[:, :n_proj]
    d_attn = jnp.dot(full_cot, w_full[:, n_proj:], preferred_element_type=jnp.float32).astype(
        jnp.bfloat16
    )
    qkv = jnp.dot(full_tokens, proj_full, preferred_element_type=jnp.float32).astype(jnp.bfloat16)
    query = qkv[:, :n_q]
    kv = qkv[:, n_q:]
    earlier = [from_behind(kv, SEQ, distance) for distance in range(reach, 0, -1)]
    kv_ext = jnp.concatenate(earlier + [kv], axis=0)
    attn, grad_q, grad_kv_ext = fused_attention(
        query, kv_ext, d_attn, block_lists, softmax_scale, head_dim
    )

    def segment(array, index):
        return array[index * tok_rows : (index + 1) * tok_rows]

    summed_kv = segment(grad_kv_ext, reach)
    for distance in range(1, reach + 1):
        summed_kv = summed_kv + from_behind(segment(grad_kv_ext, reach - distance), SEQ, -distance)
    grad_kv = summed_kv.astype(jnp.bfloat16)
    grad_act = jnp.concatenate([grad_q, grad_kv], axis=1)
    token_term = contract_cols(grad_act, proj_full).astype(jnp.bfloat16)
    n_tp = lax.psum(1, TP)
    cols = token_term.shape[1] // n_tp
    parts = lax.all_to_all(token_term.reshape(tok_rows, n_tp, cols), TP, 1, 1, tiled=True)
    grad_tokens = parts.astype(jnp.float32).sum(axis=1).astype(jnp.bfloat16)
    weight_parts = weight_terms(full_tokens.T, full_cot.T, grad_q, grad_kv, attn)
    summed = lax.psum_scatter(weight_parts, SEQ, scatter_dimension=0, tiled=True)
    grad_query = summed[:, :n_q]
    grad_key = summed[:, n_q : n_q + n_kv]
    grad_value = summed[:, n_q + n_kv : n_proj]
    grad_w_out = summed[:, n_proj:].T
    return (grad_tokens, grad_query, grad_key, grad_value, grad_w_out)


def solution(mesh):
    fine = Mesh(mesh.devices.reshape(SEQ_SPLIT + TP_SPLIT), SEQ + TP)
    in_specs = (
        P(SEQ, TP),
        P(SEQ, TP),
        P(SEQ, TP),
        P(SEQ, TP),
        P(TP, SEQ),
        P(SEQ, TP),
        P(SEQ, None),
    )
    out_specs = (P(SEQ, TP), P(SEQ, TP), P(SEQ, TP), P(SEQ, TP), P(TP, SEQ))
    return jax.shard_map(shards, mesh=fine, in_specs=in_specs, out_specs=out_specs, check_vma=False)
```

```python
import functools

import jax
import jax.numpy as jnp
from jax import lax
from jax.experimental import pallas as pl
from jax.experimental.pallas import tpu as pltpu
from jax.sharding import Mesh
from jax.sharding import PartitionSpec as P

HEADS = 32
KV_HEADS = 16
HD = 128
WIN = 1024
ATTN_SCALAR = 168

SEQ = ("ylo", "x", "core")
TP = ("z", "yhi")
SEQ_SPLIT = (2, 4, 2)
TP_SPLIT = (8, 2)


def ring_gather(block, axis, dim):
    size = lax.psum(1, axis)
    index = lax.axis_index(axis)
    right, left = [block], [block]
    for _ in range(size // 2):
        right.append(lax.ppermute(right[-1], axis, [(i, (i + 1) % size) for i in range(size)]))
    for _ in range((size - 1) // 2):
        left.append(lax.ppermute(left[-1], axis, [(i, (i - 1) % size) for i in range(size)]))
    ordered = left + [right[k] for k in range(size // 2, 0, -1)]
    shape = list(block.shape)
    shape[dim] *= size
    full = jnp.zeros(shape, block.dtype)
    for offset, piece in enumerate(ordered):
        start = [0] * len(shape)
        start[dim] = ((index + offset) % size) * block.shape[dim]
        full = lax.dynamic_update_slice(full, piece, start)
    return full


def from_behind(block, axis, distance):
    devices = range(lax.psum(1, axis))
    route = [(i - distance, i) for i in devices if i - distance in devices]
    return lax.ppermute(block, axis, route)


def _nt(left, right):
    return lax.dot_general(left, right, (((1,), (1,)), ((), ())), preferred_element_type=jnp.float32)


def _nn(left, right):
    return lax.dot_general(left, right, (((1,), (0,)), ((), ())), preferred_element_type=jnp.float32)


def attention_kernel(q_ref, d_ref, kv_ref, lst_ref, attn_ref, gq_ref, *rest, scale, block_len, span, head_dim):
    seg_refs, dkv_ref = rest[:-1], rest[-1]
    n_blocks = q_ref.shape[0] // block_len
    groups = q_ref.shape[1] // head_dim
    width = span * block_len
    dkv_ref[...] = jnp.zeros(dkv_ref.shape, jnp.float32)
    rows = lax.broadcasted_iota(jnp.int32, (block_len, width), 0)
    cols = lax.broadcasted_iota(jnp.int32, (block_len, width), 1)
    inside = (cols > rows) & (cols <= rows + (width - block_len))
    for b in range(n_blocks):
        w0 = b * block_len
        kw = kv_ref[w0 : w0 + width, :head_dim]
        vw = kv_ref[w0 : w0 + width, head_dim:]
        allowed = inside & (lst_ref[b : b + 1, :] > 0.0)
        dk_acc = jnp.zeros((width, head_dim), jnp.float32)
        dv_acc = jnp.zeros((width, head_dim), jnp.float32)
        for g in range(groups):
            r0, c0 = b * block_len, g * head_dim
            qb = q_ref[r0 : r0 + block_len, c0 : c0 + head_dim]
            db = d_ref[r0 : r0 + block_len, c0 : c0 + head_dim]
            scores = _nt(qb, kw) * scale
            masked = jnp.where(allowed, scores, -1e30)
            highest = jnp.max(masked, axis=1, keepdims=True)
            weights = jnp.where(allowed, jnp.exp(masked - highest), 0.0)
            probs = weights / jnp.sum(weights, axis=1, keepdims=True)
            probs_half = probs.astype(jnp.bfloat16)
            attn = _nn(probs_half, vw).astype(jnp.bfloat16)
            attn_ref[r0 : r0 + block_len, c0 : c0 + head_dim] = attn
            delta = jnp.sum(db.astype(jnp.float32) * attn.astype(jnp.float32), axis=1, keepdims=True)
            grad_probs = _nt(db, vw)
            grad_scores = (probs * (grad_probs - delta)).astype(jnp.bfloat16)
            grad_q = _nn(grad_scores, kw) * scale
            gq_ref[r0 : r0 + block_len, c0 : c0 + head_dim] = grad_q.astype(jnp.bfloat16)
            dk_acc = dk_acc + _nn(grad_scores.T, qb)
            dv_acc = dv_acc + _nn(probs_half.T, db)
        dkv_ref[w0 : w0 + width, :head_dim] += dk_acc * scale
        dkv_ref[w0 : w0 + width, head_dim:] += dv_acc
    seg = dkv_ref.shape[0] // len(seg_refs)
    for index, seg_ref in enumerate(seg_refs):
        seg_ref[...] = dkv_ref[index * seg : (index + 1) * seg, :]


def fused_attention(query, kv_ext, d_attn, block_lists, scale, head_dim):
    n_blocks, span = block_lists.shape
    block_len = query.shape[0] // n_blocks
    listed = jnp.repeat((block_lists >= 0).astype(jnp.float32), block_len, axis=1)
    body = functools.partial(
        attention_kernel, scale=scale, block_len=block_len, span=span, head_dim=head_dim
    )
    n_seg = kv_ext.shape[0] // query.shape[0]
    seg_shape = jax.ShapeDtypeStruct((query.shape[0], kv_ext.shape[1]), jnp.float32)
    outs = pl.pallas_call(
        body,
        out_shape=(
            jax.ShapeDtypeStruct(query.shape, jnp.bfloat16),
            jax.ShapeDtypeStruct(query.shape, jnp.bfloat16),
        )
        + (seg_shape,) * n_seg,
        scratch_shapes=[pltpu.VMEM(kv_ext.shape, jnp.float32)],
    )(query, d_attn, kv_ext, listed)
    return outs[0], outs[1], outs[2:]


def weight_terms_kernel(tok_ref, cot_ref, gq_ref, attn_ref, out_ref):
    @pl.when(pl.program_id(1) == 0)
    def _():
        out_ref[...] = _nn(tok_ref[...], gq_ref[...]).astype(out_ref.dtype)

    @pl.when(pl.program_id(1) == 1)
    def _():
        out_ref[...] = _nn(cot_ref[...], attn_ref[...]).astype(out_ref.dtype)


def kv_terms_kernel(tok_ref, gkv_ref, base_ref, out_ref):
    del base_ref
    out_ref[...] = _nn(tok_ref[...], gkv_ref[...]).astype(out_ref.dtype)


def weight_terms(tokens_t, cot_t, grad_q, grad_kv, attn, block=768):
    feats, rows = tokens_t.shape
    n_q, n_kv, n_attn = grad_q.shape[1], grad_kv.shape[1], attn.shape[1]
    width = n_q + n_kv + n_attn
    first = pl.pallas_call(
        weight_terms_kernel,
        grid=(feats // block, 2),
        in_specs=[
            pl.BlockSpec((block, rows), lambda i, j: (i, 0)),
            pl.BlockSpec((block, rows), lambda i, j: (i, 0)),
            pl.BlockSpec((rows, n_q), lambda i, j: (0, 0)),
            pl.BlockSpec((rows, n_attn), lambda i, j: (0, 0)),
        ],
        out_specs=pl.BlockSpec((block, n_q), lambda i, j: (i, 2 * j)),
        out_shape=jax.ShapeDtypeStruct((feats, width), jnp.bfloat16),
    )(tokens_t, cot_t, grad_q, attn)
    column = n_q // n_kv
    return pl.pallas_call(
        kv_terms_kernel,
        grid=(feats // block,),
        in_specs=[
            pl.BlockSpec((block, rows), lambda i: (i, 0)),
            pl.BlockSpec((rows, n_kv), lambda i: (0, 0)),
            pl.BlockSpec(memory_space=pl.ANY),
        ],
        out_specs=pl.BlockSpec((block, n_kv), lambda i: (i, column)),
        out_shape=jax.ShapeDtypeStruct((feats, width), jnp.bfloat16),
        input_output_aliases={2: 0},
    )(tokens_t, grad_kv, first)


def contract_cols(left, right):
    return lax.dot_general(
        left, right, (((1,), (1,)), ((), ())), preferred_element_type=jnp.float32
    )


def term_maker(left, right):
    return lax.dot_general(
        left, right, (((0,), (0,)), ((), ())), preferred_element_type=jnp.float32
    )


def shards(tokens, w_query, w_key, w_value, w_out, cotangent, block_lists):
    softmax_scale = ATTN_SCALAR ** (-0.5)
    head_dim = HD
    tok_rows = tokens.shape[0]
    reach = WIN // tok_rows
    n_q = w_query.shape[1]
    n_kv = w_key.shape[1]
    n_proj = n_q + 2 * n_kv
    pair = jnp.stack([tokens, cotangent])
    pair = lax.all_gather(pair, "yhi", axis=2, tiled=True)
    full_tokens = ring_gather(pair[0], "z", 1)
    full_cot = lax.all_gather(pair[1], "z", axis=1, tiled=True)
    w_cat = jnp.concatenate([w_query, w_key, w_value, w_out.T], axis=1)
    w_full = lax.all_gather(w_cat, SEQ, axis=0, tiled=True)
    proj_full = w_full[:, :n_proj]
    d_attn = jnp.dot(full_cot, w_full[:, n_proj:], preferred_element_type=jnp.float32).astype(
        jnp.bfloat16
    )
    qkv = jnp.dot(full_tokens, proj_full, preferred_element_type=jnp.float32).astype(jnp.bfloat16)
    query = qkv[:, :n_q]
    kv = qkv[:, n_q:]
    earlier = [from_behind(kv, SEQ, distance) for distance in range(reach, 0, -1)]
    kv_ext = jnp.concatenate(earlier + [kv], axis=0)
    attn, grad_q, grad_kv_ext = fused_attention(
        query, kv_ext, d_attn, block_lists, softmax_scale, head_dim
    )

    summed_kv = grad_kv_ext[reach]
    for distance in range(1, reach + 1):
        summed_kv = summed_kv + from_behind(grad_kv_ext[reach - distance], SEQ, -distance)
    grad_kv = summed_kv.astype(jnp.bfloat16)
    grad_act = jnp.concatenate([grad_q, grad_kv], axis=1)
    token_term = contract_cols(grad_act, proj_full).astype(jnp.bfloat16)
    n_tp = lax.psum(1, TP)
    cols = token_term.shape[1] // n_tp
    parts = lax.all_to_all(token_term.reshape(tok_rows, n_tp, cols), TP, 1, 1, tiled=True)
    grad_tokens = parts.astype(jnp.float32).sum(axis=1).astype(jnp.bfloat16)
    weight_parts = weight_terms(full_tokens.T, full_cot.T, grad_q, grad_kv, attn)
    summed = lax.psum_scatter(weight_parts, SEQ, scatter_dimension=0, tiled=True)
    grad_query = summed[:, :n_q]
    grad_key = summed[:, n_q : n_q + n_kv]
    grad_value = summed[:, n_q + n_kv : n_proj]
    grad_w_out = summed[:, n_proj:].T
    return (grad_tokens, grad_query, grad_key, grad_value, grad_w_out)


def solution(mesh):
    fine = Mesh(mesh.devices.reshape(SEQ_SPLIT + TP_SPLIT), SEQ + TP)
    in_specs = (
        P(SEQ, TP),
        P(SEQ, TP),
        P(SEQ, TP),
        P(SEQ, TP),
        P(TP, SEQ),
        P(SEQ, TP),
        P(SEQ, None),
    )
    out_specs = (P(SEQ, TP), P(SEQ, TP), P(SEQ, TP), P(SEQ, TP), P(TP, SEQ))
    return jax.shard_map(shards, mesh=fine, in_specs=in_specs, out_specs=out_specs, check_vma=False)
```

```python
import functools

import jax
import jax.numpy as jnp
from jax import lax
from jax.experimental import pallas as pl
from jax.experimental.pallas import tpu as pltpu
from jax.sharding import Mesh
from jax.sharding import PartitionSpec as P

HEADS = 32
KV_HEADS = 16
HD = 128
WIN = 1024
ATTN_SCALAR = 168

SEQ = ("ylo", "x", "core")
TP = ("z", "yhi")
SEQ_SPLIT = (2, 4, 2)
TP_SPLIT = (8, 2)


def ring_gather(block, axis, dim):
    size = lax.psum(1, axis)
    index = lax.axis_index(axis)
    right, left = [block], [block]
    for _ in range(size // 2):
        right.append(lax.ppermute(right[-1], axis, [(i, (i + 1) % size) for i in range(size)]))
    for _ in range((size - 1) // 2):
        left.append(lax.ppermute(left[-1], axis, [(i, (i - 1) % size) for i in range(size)]))
    ordered = left + [right[k] for k in range(size // 2, 0, -1)]
    shape = list(block.shape)
    shape[dim] *= size
    full = jnp.zeros(shape, block.dtype)
    for offset, piece in enumerate(ordered):
        start = [0] * len(shape)
        start[dim] = ((index + offset) % size) * block.shape[dim]
        full = lax.dynamic_update_slice(full, piece, start)
    return full


def from_behind(block, axis, distance):
    devices = range(lax.psum(1, axis))
    route = [(i - distance, i) for i in devices if i - distance in devices]
    return lax.ppermute(block, axis, route)


def _nt(left, right):
    return lax.dot_general(left, right, (((1,), (1,)), ((), ())), preferred_element_type=jnp.float32)


def _nn(left, right):
    return lax.dot_general(left, right, (((1,), (0,)), ((), ())), preferred_element_type=jnp.float32)


def attention_kernel(q_ref, d_ref, kv_ref, lst_ref, attn_ref, gq_ref, *rest, scale, block_len, span, head_dim):
    seg_refs, dkv_ref = rest[:-1], rest[-1]
    n_blocks = q_ref.shape[0] // block_len
    groups = q_ref.shape[1] // head_dim
    width = span * block_len
    dkv_ref[...] = jnp.zeros(dkv_ref.shape, jnp.float32)
    rows = lax.broadcasted_iota(jnp.int32, (block_len, width), 0)
    cols = lax.broadcasted_iota(jnp.int32, (block_len, width), 1)
    inside = (cols > rows) & (cols <= rows + (width - block_len))
    for b in range(n_blocks):
        w0 = b * block_len
        kw = kv_ref[w0 : w0 + width, :head_dim]
        vw = kv_ref[w0 : w0 + width, head_dim:]
        allowed = inside & (lst_ref[b : b + 1, :] > 0.0)
        dk_acc = jnp.zeros((width, head_dim), jnp.float32)
        dv_acc = jnp.zeros((width, head_dim), jnp.float32)
        for g in range(groups):
            r0, c0 = b * block_len, g * head_dim
            qb = q_ref[r0 : r0 + block_len, c0 : c0 + head_dim]
            db = d_ref[r0 : r0 + block_len, c0 : c0 + head_dim]
            scores = _nt(qb, kw) * scale
            masked = jnp.where(allowed, scores, -1e30)
            highest = jnp.max(masked, axis=1, keepdims=True)
            weights = jnp.where(allowed, jnp.exp(masked - highest), 0.0)
            probs = weights / jnp.sum(weights, axis=1, keepdims=True)
            probs_half = probs.astype(jnp.bfloat16)
            attn = _nn(probs_half, vw).astype(jnp.bfloat16)
            attn_ref[r0 : r0 + block_len, c0 : c0 + head_dim] = attn
            delta = jnp.sum(db.astype(jnp.float32) * attn.astype(jnp.float32), axis=1, keepdims=True)
            grad_probs = _nt(db, vw)
            grad_scores = (probs * (grad_probs - delta)).astype(jnp.bfloat16)
            grad_q = _nn(grad_scores, kw) * scale
            gq_ref[r0 : r0 + block_len, c0 : c0 + head_dim] = grad_q.astype(jnp.bfloat16)
            dk_acc = dk_acc + _nn(grad_scores.T, qb)
            dv_acc = dv_acc + _nn(probs_half.T, db)
        dkv_ref[w0 : w0 + width, :head_dim] += dk_acc * scale
        dkv_ref[w0 : w0 + width, head_dim:] += dv_acc
    seg = dkv_ref.shape[0] // len(seg_refs)
    for index, seg_ref in enumerate(seg_refs):
        seg_ref[...] = dkv_ref[index * seg : (index + 1) * seg, :]


def fused_attention(query, kv_ext, d_attn, block_lists, scale, head_dim):
    n_blocks, span = block_lists.shape
    block_len = query.shape[0] // n_blocks
    listed = jnp.repeat((block_lists >= 0).astype(jnp.float32), block_len, axis=1)
    body = functools.partial(
        attention_kernel, scale=scale, block_len=block_len, span=span, head_dim=head_dim
    )
    n_seg = kv_ext.shape[0] // query.shape[0]
    seg_shape = jax.ShapeDtypeStruct((query.shape[0], kv_ext.shape[1]), jnp.float32)
    outs = pl.pallas_call(
        body,
        out_shape=(
            jax.ShapeDtypeStruct(query.shape, jnp.bfloat16),
            jax.ShapeDtypeStruct(query.shape, jnp.bfloat16),
        )
        + (seg_shape,) * n_seg,
        scratch_shapes=[pltpu.VMEM(kv_ext.shape, jnp.float32)],
    )(query, d_attn, kv_ext, listed)
    return outs[0], outs[1], outs[2:]


def weight_terms_kernel(tok_ref, cot_ref, gq_ref, attn_ref, out_ref):
    n_q = gq_ref.shape[1]
    n_attn = attn_ref.shape[1]
    width = out_ref.shape[1]
    out_ref[:, :n_q] = _nn(tok_ref[...], gq_ref[...]).astype(out_ref.dtype)
    out_ref[:, width - n_attn :] = _nn(cot_ref[...], attn_ref[...]).astype(out_ref.dtype)


def kv_terms_kernel(tok_ref, gkv_ref, base_ref, out_ref):
    del base_ref
    out_ref[...] = _nn(tok_ref[...], gkv_ref[...]).astype(out_ref.dtype)


def weight_terms(tokens_t, cot_t, grad_q, grad_kv, attn, block=768):
    feats, rows = tokens_t.shape
    n_q, n_kv, n_attn = grad_q.shape[1], grad_kv.shape[1], attn.shape[1]
    width = n_q + n_kv + n_attn
    first = pl.pallas_call(
        weight_terms_kernel,
        grid=(feats // block,),
        in_specs=[
            pl.BlockSpec((block, rows), lambda i: (i, 0)),
            pl.BlockSpec((block, rows), lambda i: (i, 0)),
            pl.BlockSpec((rows, n_q), lambda i: (0, 0)),
            pl.BlockSpec((rows, n_attn), lambda i: (0, 0)),
        ],
        out_specs=pl.BlockSpec((block, width), lambda i: (i, 0)),
        out_shape=jax.ShapeDtypeStruct((feats, width), jnp.bfloat16),
    )(tokens_t, cot_t, grad_q, attn)
    column = n_q // n_kv
    return pl.pallas_call(
        kv_terms_kernel,
        grid=(feats // block,),
        in_specs=[
            pl.BlockSpec((block, rows), lambda i: (i, 0)),
            pl.BlockSpec((rows, n_kv), lambda i: (0, 0)),
            pl.BlockSpec(memory_space=pl.ANY),
        ],
        out_specs=pl.BlockSpec((block, n_kv), lambda i: (i, column)),
        out_shape=jax.ShapeDtypeStruct((feats, width), jnp.bfloat16),
        input_output_aliases={2: 0},
    )(tokens_t, grad_kv, first)


def contract_cols(left, right):
    return lax.dot_general(
        left, right, (((1,), (1,)), ((), ())), preferred_element_type=jnp.float32
    )


def term_maker(left, right):
    return lax.dot_general(
        left, right, (((0,), (0,)), ((), ())), preferred_element_type=jnp.float32
    )


def shards(tokens, w_query, w_key, w_value, w_out, cotangent, block_lists):
    softmax_scale = ATTN_SCALAR ** (-0.5)
    head_dim = HD
    tok_rows = tokens.shape[0]
    reach = WIN // tok_rows
    n_q = w_query.shape[1]
    n_kv = w_key.shape[1]
    n_proj = n_q + 2 * n_kv
    pair = jnp.stack([tokens, cotangent])
    pair = lax.all_gather(pair, "yhi", axis=2, tiled=True)
    full_tokens = ring_gather(pair[0], "z", 1)
    full_cot = lax.all_gather(pair[1], "z", axis=1, tiled=True)
    w_cat = jnp.concatenate([w_query, w_key, w_value, w_out.T], axis=1)
    w_full = lax.all_gather(w_cat, SEQ, axis=0, tiled=True)
    proj_full = w_full[:, :n_proj]
    d_attn = jnp.dot(full_cot, w_full[:, n_proj:], preferred_element_type=jnp.float32).astype(
        jnp.bfloat16
    )
    qkv = jnp.dot(full_tokens, proj_full, preferred_element_type=jnp.float32).astype(jnp.bfloat16)
    query = qkv[:, :n_q]
    kv = qkv[:, n_q:]
    earlier = [from_behind(kv, SEQ, distance) for distance in range(reach, 0, -1)]
    kv_ext = jnp.concatenate(earlier + [kv], axis=0)
    attn, grad_q, grad_kv_ext = fused_attention(
        query, kv_ext, d_attn, block_lists, softmax_scale, head_dim
    )

    summed_kv = grad_kv_ext[reach]
    for distance in range(1, reach + 1):
        summed_kv = summed_kv + from_behind(grad_kv_ext[reach - distance], SEQ, -distance)
    grad_kv = summed_kv.astype(jnp.bfloat16)
    grad_act = jnp.concatenate([grad_q, grad_kv], axis=1)
    token_term = contract_cols(grad_act, proj_full).astype(jnp.bfloat16)
    n_tp = lax.psum(1, TP)
    cols = token_term.shape[1] // n_tp
    parts = lax.all_to_all(token_term.reshape(tok_rows, n_tp, cols), TP, 1, 1, tiled=True)
    grad_tokens = parts.astype(jnp.float32).sum(axis=1).astype(jnp.bfloat16)
    weight_parts = weight_terms(full_tokens.T, full_cot.T, grad_q, grad_kv, attn)
    summed = lax.psum_scatter(weight_parts, SEQ, scatter_dimension=0, tiled=True)
    grad_query = summed[:, :n_q]
    grad_key = summed[:, n_q : n_q + n_kv]
    grad_value = summed[:, n_q + n_kv : n_proj]
    grad_w_out = summed[:, n_proj:].T
    return (grad_tokens, grad_query, grad_key, grad_value, grad_w_out)


def solution(mesh):
    fine = Mesh(mesh.devices.reshape(SEQ_SPLIT + TP_SPLIT), SEQ + TP)
    in_specs = (
        P(SEQ, TP),
        P(SEQ, TP),
        P(SEQ, TP),
        P(SEQ, TP),
        P(TP, SEQ),
        P(SEQ, TP),
        P(SEQ, None),
    )
    out_specs = (P(SEQ, TP), P(SEQ, TP), P(SEQ, TP), P(SEQ, TP), P(TP, SEQ))
    return jax.shard_map(shards, mesh=fine, in_specs=in_specs, out_specs=out_specs, check_vma=False)
```

```python
import functools

import jax
import jax.numpy as jnp
from jax import lax
from jax.experimental import pallas as pl
from jax.experimental.pallas import tpu as pltpu
from jax.sharding import Mesh
from jax.sharding import PartitionSpec as P

HEADS = 32
KV_HEADS = 16
HD = 128
WIN = 1024
ATTN_SCALAR = 168

SEQ = ("ylo", "x", "core")
TP = ("z", "yhi")
SEQ_SPLIT = (2, 4, 2)
TP_SPLIT = (8, 2)


def ring_gather(block, axis, dim):
    size = lax.psum(1, axis)
    index = lax.axis_index(axis)
    right, left = [block], [block]
    for _ in range(size // 2):
        right.append(lax.ppermute(right[-1], axis, [(i, (i + 1) % size) for i in range(size)]))
    for _ in range((size - 1) // 2):
        left.append(lax.ppermute(left[-1], axis, [(i, (i - 1) % size) for i in range(size)]))
    ordered = left + [right[k] for k in range(size // 2, 0, -1)]
    shape = list(block.shape)
    shape[dim] *= size
    full = jnp.zeros(shape, block.dtype)
    for offset, piece in enumerate(ordered):
        start = [0] * len(shape)
        start[dim] = ((index + offset) % size) * block.shape[dim]
        full = lax.dynamic_update_slice(full, piece, start)
    return full


def from_behind(block, axis, distance):
    devices = range(lax.psum(1, axis))
    route = [(i - distance, i) for i in devices if i - distance in devices]
    return lax.ppermute(block, axis, route)


def _nt(left, right):
    return lax.dot_general(left, right, (((1,), (1,)), ((), ())), preferred_element_type=jnp.float32)


def _nn(left, right):
    return lax.dot_general(left, right, (((1,), (0,)), ((), ())), preferred_element_type=jnp.float32)


def attention_kernel(q_ref, cot_ref, wo_ref, kv_ref, lst_ref, attn_ref, gq_ref, *rest, scale, block_len, span, head_dim):
    seg_refs, dkv_ref = rest[:-1], rest[-1]
    n_blocks = q_ref.shape[0] // block_len
    d_all = _nn(cot_ref[...], wo_ref[...]).astype(jnp.bfloat16)
    groups = q_ref.shape[1] // head_dim
    width = span * block_len
    dkv_ref[...] = jnp.zeros(dkv_ref.shape, jnp.float32)
    rows = lax.broadcasted_iota(jnp.int32, (block_len, width), 0)
    cols = lax.broadcasted_iota(jnp.int32, (block_len, width), 1)
    inside = (cols > rows) & (cols <= rows + (width - block_len))
    for b in range(n_blocks):
        w0 = b * block_len
        kw = kv_ref[w0 : w0 + width, :head_dim]
        vw = kv_ref[w0 : w0 + width, head_dim:]
        allowed = inside & (lst_ref[b : b + 1, :] > 0.0)
        dk_acc = jnp.zeros((width, head_dim), jnp.float32)
        dv_acc = jnp.zeros((width, head_dim), jnp.float32)
        for g in range(groups):
            r0, c0 = b * block_len, g * head_dim
            qb = q_ref[r0 : r0 + block_len, c0 : c0 + head_dim]
            db = d_all[r0 : r0 + block_len, c0 : c0 + head_dim]
            scores = _nt(qb, kw) * scale
            masked = jnp.where(allowed, scores, -1e30)
            highest = jnp.max(masked, axis=1, keepdims=True)
            weights = jnp.where(allowed, jnp.exp(masked - highest), 0.0)
            probs = weights / jnp.sum(weights, axis=1, keepdims=True)
            probs_half = probs.astype(jnp.bfloat16)
            attn = _nn(probs_half, vw).astype(jnp.bfloat16)
            attn_ref[r0 : r0 + block_len, c0 : c0 + head_dim] = attn
            delta = jnp.sum(db.astype(jnp.float32) * attn.astype(jnp.float32), axis=1, keepdims=True)
            grad_probs = _nt(db, vw)
            grad_scores = (probs * (grad_probs - delta)).astype(jnp.bfloat16)
            grad_q = _nn(grad_scores, kw) * scale
            gq_ref[r0 : r0 + block_len, c0 : c0 + head_dim] = grad_q.astype(jnp.bfloat16)
            dk_acc = dk_acc + _nn(grad_scores.T, qb)
            dv_acc = dv_acc + _nn(probs_half.T, db)
        dkv_ref[w0 : w0 + width, :head_dim] += dk_acc * scale
        dkv_ref[w0 : w0 + width, head_dim:] += dv_acc
    seg = dkv_ref.shape[0] // len(seg_refs)
    for index, seg_ref in enumerate(seg_refs):
        seg_ref[...] = dkv_ref[index * seg : (index + 1) * seg, :]


def fused_attention(query, kv_ext, full_cot, wo_t, block_lists, scale, head_dim):
    n_blocks, span = block_lists.shape
    block_len = query.shape[0] // n_blocks
    listed = jnp.repeat((block_lists >= 0).astype(jnp.float32), block_len, axis=1)
    body = functools.partial(
        attention_kernel, scale=scale, block_len=block_len, span=span, head_dim=head_dim
    )
    n_seg = kv_ext.shape[0] // query.shape[0]
    seg_shape = jax.ShapeDtypeStruct((query.shape[0], kv_ext.shape[1]), jnp.float32)
    outs = pl.pallas_call(
        body,
        out_shape=(
            jax.ShapeDtypeStruct(query.shape, jnp.bfloat16),
            jax.ShapeDtypeStruct(query.shape, jnp.bfloat16),
        )
        + (seg_shape,) * n_seg,
        scratch_shapes=[pltpu.VMEM(kv_ext.shape, jnp.float32)],
    )(query, full_cot, wo_t, kv_ext, listed)
    return outs[0], outs[1], outs[2:]


def weight_terms_kernel(tok_ref, cot_ref, gq_ref, attn_ref, out_ref):
    n_q = gq_ref.shape[1]
    n_attn = attn_ref.shape[1]
    width = out_ref.shape[1]
    out_ref[:, :n_q] = _nn(tok_ref[...], gq_ref[...]).astype(out_ref.dtype)
    out_ref[:, width - n_attn :] = _nn(cot_ref[...], attn_ref[...]).astype(out_ref.dtype)


def kv_terms_kernel(tok_ref, gkv_ref, base_ref, out_ref):
    del base_ref
    out_ref[...] = _nn(tok_ref[...], gkv_ref[...]).astype(out_ref.dtype)


def weight_terms(tokens_t, cot_t, grad_q, grad_kv, attn, block=768):
    feats, rows = tokens_t.shape
    n_q, n_kv, n_attn = grad_q.shape[1], grad_kv.shape[1], attn.shape[1]
    width = n_q + n_kv + n_attn
    first = pl.pallas_call(
        weight_terms_kernel,
        grid=(feats // block,),
        in_specs=[
            pl.BlockSpec((block, rows), lambda i: (i, 0)),
            pl.BlockSpec((block, rows), lambda i: (i, 0)),
            pl.BlockSpec((rows, n_q), lambda i: (0, 0)),
            pl.BlockSpec((rows, n_attn), lambda i: (0, 0)),
        ],
        out_specs=pl.BlockSpec((block, width), lambda i: (i, 0)),
        out_shape=jax.ShapeDtypeStruct((feats, width), jnp.bfloat16),
    )(tokens_t, cot_t, grad_q, attn)
    column = n_q // n_kv
    return pl.pallas_call(
        kv_terms_kernel,
        grid=(feats // block,),
        in_specs=[
            pl.BlockSpec((block, rows), lambda i: (i, 0)),
            pl.BlockSpec((rows, n_kv), lambda i: (0, 0)),
            pl.BlockSpec(memory_space=pl.ANY),
        ],
        out_specs=pl.BlockSpec((block, n_kv), lambda i: (i, column)),
        out_shape=jax.ShapeDtypeStruct((feats, width), jnp.bfloat16),
        input_output_aliases={2: 0},
    )(tokens_t, grad_kv, first)


def contract_cols(left, right):
    return lax.dot_general(
        left, right, (((1,), (1,)), ((), ())), preferred_element_type=jnp.float32
    )


def term_maker(left, right):
    return lax.dot_general(
        left, right, (((0,), (0,)), ((), ())), preferred_element_type=jnp.float32
    )


def shards(tokens, w_query, w_key, w_value, w_out, cotangent, block_lists):
    softmax_scale = ATTN_SCALAR ** (-0.5)
    head_dim = HD
    tok_rows = tokens.shape[0]
    reach = WIN // tok_rows
    n_q = w_query.shape[1]
    n_kv = w_key.shape[1]
    n_proj = n_q + 2 * n_kv
    pair = jnp.stack([tokens, cotangent])
    pair = lax.all_gather(pair, "yhi", axis=2, tiled=True)
    full_tokens = ring_gather(pair[0], "z", 1)
    full_cot = lax.all_gather(pair[1], "z", axis=1, tiled=True)
    w_cat = jnp.concatenate([w_query, w_key, w_value, w_out.T], axis=1)
    w_full = lax.all_gather(w_cat, SEQ, axis=0, tiled=True)
    proj_full = w_full[:, :n_proj]
    qkv = jnp.dot(full_tokens, proj_full, preferred_element_type=jnp.float32).astype(jnp.bfloat16)
    query = qkv[:, :n_q]
    kv = qkv[:, n_q:]
    earlier = [from_behind(kv, SEQ, distance) for distance in range(reach, 0, -1)]
    kv_ext = jnp.concatenate(earlier + [kv], axis=0)
    attn, grad_q, grad_kv_ext = fused_attention(
        query, kv_ext, full_cot, w_full[:, n_proj:], block_lists, softmax_scale, head_dim
    )

    summed_kv = grad_kv_ext[reach]
    for distance in range(1, reach + 1):
        summed_kv = summed_kv + from_behind(grad_kv_ext[reach - distance], SEQ, -distance)
    grad_kv = summed_kv.astype(jnp.bfloat16)
    grad_act = jnp.concatenate([grad_q, grad_kv], axis=1)
    token_term = contract_cols(grad_act, proj_full).astype(jnp.bfloat16)
    n_tp = lax.psum(1, TP)
    cols = token_term.shape[1] // n_tp
    parts = lax.all_to_all(token_term.reshape(tok_rows, n_tp, cols), TP, 1, 1, tiled=True)
    grad_tokens = parts.astype(jnp.float32).sum(axis=1).astype(jnp.bfloat16)
    weight_parts = weight_terms(full_tokens.T, full_cot.T, grad_q, grad_kv, attn)
    summed = lax.psum_scatter(weight_parts, SEQ, scatter_dimension=0, tiled=True)
    grad_query = summed[:, :n_q]
    grad_key = summed[:, n_q : n_q + n_kv]
    grad_value = summed[:, n_q + n_kv : n_proj]
    grad_w_out = summed[:, n_proj:].T
    return (grad_tokens, grad_query, grad_key, grad_value, grad_w_out)


def solution(mesh):
    fine = Mesh(mesh.devices.reshape(SEQ_SPLIT + TP_SPLIT), SEQ + TP)
    in_specs = (
        P(SEQ, TP),
        P(SEQ, TP),
        P(SEQ, TP),
        P(SEQ, TP),
        P(TP, SEQ),
        P(SEQ, TP),
        P(SEQ, None),
    )
    out_specs = (P(SEQ, TP), P(SEQ, TP), P(SEQ, TP), P(SEQ, TP), P(TP, SEQ))
    return jax.shard_map(shards, mesh=fine, in_specs=in_specs, out_specs=out_specs, check_vma=False)
```

```python
import functools

import jax
import jax.numpy as jnp
from jax import lax
from jax.experimental import pallas as pl
from jax.experimental.pallas import tpu as pltpu
from jax.sharding import Mesh
from jax.sharding import PartitionSpec as P

HEADS = 32
KV_HEADS = 16
HD = 128
WIN = 1024
ATTN_SCALAR = 168

SEQ = ("ylo", "x", "core")
TP = ("z", "yhi")
SEQ_SPLIT = (2, 4, 2)
TP_SPLIT = (8, 2)


def ring_gather(block, axis, dim):
    size = lax.psum(1, axis)
    index = lax.axis_index(axis)
    right, left = [block], [block]
    for _ in range(size // 2):
        right.append(lax.ppermute(right[-1], axis, [(i, (i + 1) % size) for i in range(size)]))
    for _ in range((size - 1) // 2):
        left.append(lax.ppermute(left[-1], axis, [(i, (i - 1) % size) for i in range(size)]))
    ordered = left + [right[k] for k in range(size // 2, 0, -1)]
    shape = list(block.shape)
    shape[dim] *= size
    full = jnp.zeros(shape, block.dtype)
    for offset, piece in enumerate(ordered):
        start = [0] * len(shape)
        start[dim] = ((index + offset) % size) * block.shape[dim]
        full = lax.dynamic_update_slice(full, piece, start)
    return full


def from_behind(block, axis, distance):
    devices = range(lax.psum(1, axis))
    route = [(i - distance, i) for i in devices if i - distance in devices]
    return lax.ppermute(block, axis, route)


def _nt(left, right):
    return lax.dot_general(left, right, (((1,), (1,)), ((), ())), preferred_element_type=jnp.float32)


def _nn(left, right):
    return lax.dot_general(left, right, (((1,), (0,)), ((), ())), preferred_element_type=jnp.float32)


def attention_kernel(q_ref, d_ref, kv_ref, lst_ref, attn_ref, gq_ref, *rest, scale, block_len, span, head_dim):
    seg_refs, dkv_ref = rest[:-1], rest[-1]
    n_blocks = q_ref.shape[0] // block_len
    groups = q_ref.shape[1] // head_dim
    width = span * block_len
    dkv_ref[...] = jnp.zeros(dkv_ref.shape, jnp.float32)
    rows = lax.broadcasted_iota(jnp.int32, (block_len, width), 0)
    cols = lax.broadcasted_iota(jnp.int32, (block_len, width), 1)
    inside = (cols > rows) & (cols <= rows + (width - block_len))
    for b in range(n_blocks):
        w0 = b * block_len
        kw = kv_ref[w0 : w0 + width, :head_dim]
        vw = kv_ref[w0 : w0 + width, head_dim:]
        allowed = inside & (lst_ref[b : b + 1, :] > 0.0)
        dk_acc = jnp.zeros((width, head_dim), jnp.float32)
        dv_acc = jnp.zeros((width, head_dim), jnp.float32)
        for g in range(groups):
            r0, c0 = b * block_len, g * head_dim
            qb = q_ref[r0 : r0 + block_len, c0 : c0 + head_dim]
            db = d_ref[r0 : r0 + block_len, c0 : c0 + head_dim]
            scores = _nt(qb, kw) * scale
            masked = jnp.where(allowed, scores, -1e30)
            highest = jnp.max(masked, axis=1, keepdims=True)
            weights = jnp.where(allowed, jnp.exp(masked - highest), 0.0)
            probs = weights / jnp.sum(weights, axis=1, keepdims=True)
            probs_half = probs.astype(jnp.bfloat16)
            attn = _nn(probs_half, vw).astype(jnp.bfloat16)
            attn_ref[r0 : r0 + block_len, c0 : c0 + head_dim] = attn
            delta = jnp.sum(db.astype(jnp.float32) * attn.astype(jnp.float32), axis=1, keepdims=True)
            grad_probs = _nt(db, vw)
            grad_scores = (probs * (grad_probs - delta)).astype(jnp.bfloat16)
            grad_q = _nn(grad_scores, kw) * scale
            gq_ref[r0 : r0 + block_len, c0 : c0 + head_dim] = grad_q.astype(jnp.bfloat16)
            dk_acc = dk_acc + _nn(grad_scores.T, qb)
            dv_acc = dv_acc + _nn(probs_half.T, db)
        dkv_ref[w0 : w0 + width, :head_dim] += dk_acc * scale
        dkv_ref[w0 : w0 + width, head_dim:] += dv_acc
    seg = dkv_ref.shape[0] // len(seg_refs)
    for index, seg_ref in enumerate(seg_refs):
        seg_ref[...] = dkv_ref[index * seg : (index + 1) * seg, :]


def fused_attention(query, kv_ext, d_attn, block_lists, scale, head_dim):
    n_blocks, span = block_lists.shape
    block_len = query.shape[0] // n_blocks
    listed = jnp.repeat((block_lists >= 0).astype(jnp.float32), block_len, axis=1)
    body = functools.partial(
        attention_kernel, scale=scale, block_len=block_len, span=span, head_dim=head_dim
    )
    n_seg = kv_ext.shape[0] // query.shape[0]
    seg_shape = jax.ShapeDtypeStruct((query.shape[0], kv_ext.shape[1]), jnp.float32)
    outs = pl.pallas_call(
        body,
        out_shape=(
            jax.ShapeDtypeStruct(query.shape, jnp.bfloat16),
            jax.ShapeDtypeStruct(query.shape, jnp.bfloat16),
        )
        + (seg_shape,) * n_seg,
        scratch_shapes=[pltpu.VMEM(kv_ext.shape, jnp.float32)],
    )(query, d_attn, kv_ext, listed)
    return outs[0], outs[1], outs[2:]


def weight_terms_kernel(tok_ref, cot_ref, gq_ref, attn_ref, out_ref):
    n_q = gq_ref.shape[1]
    n_attn = attn_ref.shape[1]
    width = out_ref.shape[1]
    out_ref[:, :n_q] = _nn(tok_ref[...], gq_ref[...]).astype(out_ref.dtype)
    out_ref[:, width - n_attn :] = _nn(cot_ref[...], attn_ref[...]).astype(out_ref.dtype)


def kv_terms_kernel(tok_ref, gkv_ref, base_ref, out_ref):
    del base_ref
    out_ref[...] = _nn(tok_ref[...], gkv_ref[...]).astype(out_ref.dtype)


def weight_terms(tokens_t, cot_t, grad_q, grad_kv, attn, block=1344):
    feats, rows = tokens_t.shape
    n_q, n_kv, n_attn = grad_q.shape[1], grad_kv.shape[1], attn.shape[1]
    width = n_q + n_kv + n_attn
    first = pl.pallas_call(
        weight_terms_kernel,
        grid=(feats // block,),
        in_specs=[
            pl.BlockSpec((block, rows), lambda i: (i, 0)),
            pl.BlockSpec((block, rows), lambda i: (i, 0)),
            pl.BlockSpec((rows, n_q), lambda i: (0, 0)),
            pl.BlockSpec((rows, n_attn), lambda i: (0, 0)),
        ],
        out_specs=pl.BlockSpec((block, width), lambda i: (i, 0)),
        out_shape=jax.ShapeDtypeStruct((feats, width), jnp.bfloat16),
    )(tokens_t, cot_t, grad_q, attn)
    column = n_q // n_kv
    return pl.pallas_call(
        kv_terms_kernel,
        grid=(feats // block,),
        in_specs=[
            pl.BlockSpec((block, rows), lambda i: (i, 0)),
            pl.BlockSpec((rows, n_kv), lambda i: (0, 0)),
            pl.BlockSpec(memory_space=pl.ANY),
        ],
        out_specs=pl.BlockSpec((block, n_kv), lambda i: (i, column)),
        out_shape=jax.ShapeDtypeStruct((feats, width), jnp.bfloat16),
        input_output_aliases={2: 0},
    )(tokens_t, grad_kv, first)


def contract_cols(left, right):
    return lax.dot_general(
        left, right, (((1,), (1,)), ((), ())), preferred_element_type=jnp.float32
    )


def term_maker(left, right):
    return lax.dot_general(
        left, right, (((0,), (0,)), ((), ())), preferred_element_type=jnp.float32
    )


def shards(tokens, w_query, w_key, w_value, w_out, cotangent, block_lists):
    softmax_scale = ATTN_SCALAR ** (-0.5)
    head_dim = HD
    tok_rows = tokens.shape[0]
    reach = WIN // tok_rows
    n_q = w_query.shape[1]
    n_kv = w_key.shape[1]
    n_proj = n_q + 2 * n_kv
    pair = jnp.stack([tokens, cotangent])
    pair = lax.all_gather(pair, "yhi", axis=2, tiled=True)
    full_tokens = ring_gather(pair[0], "z", 1)
    full_cot = lax.all_gather(pair[1], "z", axis=1, tiled=True)
    w_cat = jnp.concatenate([w_query, w_key, w_value, w_out.T], axis=1)
    w_full = lax.all_gather(w_cat, SEQ, axis=0, tiled=True)
    proj_full = w_full[:, :n_proj]
    d_attn = jnp.dot(full_cot, w_full[:, n_proj:], preferred_element_type=jnp.float32).astype(
        jnp.bfloat16
    )
    qkv = jnp.dot(full_tokens, proj_full, preferred_element_type=jnp.float32).astype(jnp.bfloat16)
    query = qkv[:, :n_q]
    kv = qkv[:, n_q:]
    earlier = [from_behind(kv, SEQ, distance) for distance in range(reach, 0, -1)]
    kv_ext = jnp.concatenate(earlier + [kv], axis=0)
    attn, grad_q, grad_kv_ext = fused_attention(
        query, kv_ext, d_attn, block_lists, softmax_scale, head_dim
    )

    summed_kv = grad_kv_ext[reach]
    for distance in range(1, reach + 1):
        summed_kv = summed_kv + from_behind(grad_kv_ext[reach - distance], SEQ, -distance)
    grad_kv = summed_kv.astype(jnp.bfloat16)
    grad_act = jnp.concatenate([grad_q, grad_kv], axis=1)
    token_term = contract_cols(grad_act, proj_full).astype(jnp.bfloat16)
    n_tp = lax.psum(1, TP)
    cols = token_term.shape[1] // n_tp
    parts = lax.all_to_all(token_term.reshape(tok_rows, n_tp, cols), TP, 1, 1, tiled=True)
    grad_tokens = parts.astype(jnp.float32).sum(axis=1).astype(jnp.bfloat16)
    weight_parts = weight_terms(full_tokens.T, full_cot.T, grad_q, grad_kv, attn)
    summed = lax.psum_scatter(weight_parts, SEQ, scatter_dimension=0, tiled=True)
    grad_query = summed[:, :n_q]
    grad_key = summed[:, n_q : n_q + n_kv]
    grad_value = summed[:, n_q + n_kv : n_proj]
    grad_w_out = summed[:, n_proj:].T
    return (grad_tokens, grad_query, grad_key, grad_value, grad_w_out)


def solution(mesh):
    fine = Mesh(mesh.devices.reshape(SEQ_SPLIT + TP_SPLIT), SEQ + TP)
    in_specs = (
        P(SEQ, TP),
        P(SEQ, TP),
        P(SEQ, TP),
        P(SEQ, TP),
        P(TP, SEQ),
        P(SEQ, TP),
        P(SEQ, None),
    )
    out_specs = (P(SEQ, TP), P(SEQ, TP), P(SEQ, TP), P(SEQ, TP), P(TP, SEQ))
    return jax.shard_map(shards, mesh=fine, in_specs=in_specs, out_specs=out_specs, check_vma=False)
```
